128 devices in a mesh: path: 16 (over x_hi, y, core), shard: 8 (over x_lo, z).
Axes of the slice: x: 4 (x_hi: 2, x_lo: 2; x = x_hi * 2 + x_lo), y: 4, z: 4, core: 2. Of those that a mesh axis runs over, the one named last changes fastest.
Arguments:
- path_params: bfloat16 [16, 16, 64, 4096], P('path', None, 'shard'), may hold values from -6 to 6
- global_params: float32 [256, 64, 4096], P('path', 'shard'), may hold values from -6 to 6
- momentum: float32 [256, 64, 4096], P('path', 'shard'), may hold values from -6 to 6
- module_ids: int32 [16, 16], replicated, may hold values from 0 to 255, as said below
- token_counts: int32 [16, 16], replicated, may hold values from 16 to 256
Outputs:
- new_global: float32 [256, 64, 4096], P('path', 'shard')
- new_momentum: float32 [256, 64, 4096], P('path', 'shard')
- path_modules: bfloat16 [16, 16, 64, 4096], P('path', None, 'shard')
The draws below stay inside these ranges and needn't reach their ends.
Inputs may be any that keep to these rules, and one draw needn't show every extreme that they name: `module_ids`: each row names 16 different modules. Among the modules of one row, at most 2 lie in any one block of 16 consecutive module numbers, and every row has exactly 2 in some block.
All inputs are finite; a program needn't handle non-finite values.
Results may differ from the reference program's by a relative error of at most 0.0004.
Values may be sent and summed in bfloat16 or wider, within the bound.
A program may use at most 128 MiB of HBM per device.

```python
import jax
import jax.numpy as jnp
from jax import lax

D = 4096
OWNED = 16
HELD = 16
PATHS = 16
MODULES = 256
ROWS = 64


def draw_module_ids(key, part):
    base = jax.random.fold_in(key, 11)
    popular = jax.random.randint(jax.random.fold_in(base, 1), (PATHS, OWNED), 0, 4)

    def one_path(index):
        path_key = jax.random.fold_in(base, 100 + index)
        pool = jnp.arange(2 * PATHS, dtype=jnp.int32) % PATHS
        chosen = jax.random.permutation(jax.random.fold_in(path_key, 1), pool)[:HELD]
        first_count = jnp.sum((chosen[:HELD - 1] == chosen[0]).astype(jnp.int32))
        last = jnp.where(first_count == 1, chosen[0], chosen[HELD - 1])
        chosen = chosen.at[HELD - 1].set(last)
        places = jnp.arange(HELD, dtype=jnp.int32)
        before = (chosen[None, :] == chosen[:, None]) & (places[None, :] < places[:, None])
        earlier = jnp.sum(before.astype(jnp.int32), axis=1)
        noise = jax.random.randint(jax.random.fold_in(path_key, 2), (PATHS, OWNED), 0, 1024)
        scores = (noise + popular * 1024) * OWNED + jnp.arange(OWNED, dtype=jnp.int32)[None, :]
        order = jnp.argsort(-scores, axis=1, stable=True).astype(jnp.int32)
        local = order[chosen, earlier]
        return (chosen * OWNED + local).astype(jnp.int32)
    return jax.vmap(one_path)(jnp.arange(PATHS, dtype=jnp.int32))


def place_ends(entries, rng, smallest, largest):
    dims = entries.shape
    spot = [jax.random.randint(jax.random.fold_in(rng, axis), (), 0, dims[axis]) for axis in range(len(dims))]
    entries = entries.at[tuple(spot)].set(smallest)
    longest = dims.index(max(dims))
    spot[longest] = (spot[longest] + 1) % dims[longest]
    return entries.at[tuple(spot)].set(largest)


def shard_levels(rng, extent, pieces, low, largest):
    gain = 1.0
    for axis_at, blocks in pieces:
        draws = jax.random.uniform(jax.random.fold_in(jax.random.fold_in(rng, 6), axis_at), (blocks,), jnp.float32, low / len(pieces), largest / len(pieces))
        gain = gain * jnp.repeat(jnp.exp(draws), extent[axis_at] // blocks).reshape((-1,) + (1,) * (len(extent) - 1 - axis_at))
    return gain


def gaussian(own_key, dims, width, limit, split=(), kind=jnp.bfloat16):
    drawn = width * jax.random.normal(own_key, dims, jnp.float32)
    if split:
        drawn = drawn * shard_levels(own_key, dims, split, -0.22, 0.18)
    return jnp.clip(drawn, -limit, limit).astype(kind)


def setup_inputs(seed: int = 0) -> dict:
    splits = jax.random.split(jax.random.key(seed), 6)
    path_params = gaussian(splits[0], (PATHS, HELD, ROWS, D), 1.0, 6.0, ((0, 16), (2, 8)))
    global_params = gaussian(splits[1], (MODULES, ROWS, D), 1.0, 6.0, ((0, 16), (1, 8)), jnp.float32)
    momentum = gaussian(splits[2], (MODULES, ROWS, D), 1.0, 6.0, ((0, 16), (1, 8)), jnp.float32)
    module_ids = draw_module_ids(jax.random.fold_in(splits[5], 71), 0)
    token_counts = place_ends(jax.random.randint(splits[4], (PATHS, HELD), 16, 257), jax.random.fold_in(splits[4], 1), 16, 256).astype(jnp.int32)
    return dict(path_params=path_params, global_params=global_params, momentum=momentum, module_ids=module_ids, token_counts=token_counts)


outer_momentum = 0.9
outer_rate = 0.7

def reference(path_params, global_params, momentum, module_ids, token_counts):
    flat = path_params.reshape(PATHS * HELD, ROWS * D).astype(jnp.float32)
    flat_ids = module_ids.reshape(-1)
    flat_counts = token_counts.reshape(-1).astype(jnp.float32)
    targets = jnp.arange(MODULES, dtype=jnp.int32)
    weights = jnp.where(flat_ids[None, :] == targets[:, None], flat_counts[None, :], jnp.float32(0.0))
    total = lax.optimization_barrier(jnp.sum(weights, axis=1))
    summed = jnp.dot(weights, flat, precision=lax.Precision.HIGHEST)
    params = global_params.reshape(MODULES, ROWS * D)
    past = momentum.reshape(MODULES, ROWS * D)
    raw = (total[:, None] * params - summed) / jnp.maximum(total, 1.0)[:, None]
    factor = jnp.minimum(1.0, 1.0 / jnp.sqrt(lax.optimization_barrier(jnp.mean(raw * raw, axis=1)) + 1e-06))
    delta = raw * factor[:, None]
    velocity = outer_momentum * past + delta
    updated = params - outer_rate * (outer_momentum * velocity + delta)
    rounded = updated.astype(jnp.bfloat16)
    picked = rounded[flat_ids]
    return (updated.reshape(MODULES, ROWS, D), velocity.reshape(MODULES, ROWS, D), picked.reshape(PATHS, HELD, ROWS, D))
```

```python
import functools

import jax
import jax.numpy as jnp
from jax import lax
from jax.experimental import pallas as pl
from jax.experimental.pallas import tpu as pltpu
from jax.sharding import PartitionSpec as P

MESH = pl.DeviceIdType.MESH
CAP = 2
CHUNKS = 4
LANES = 128

outer_momentum = 0.9
outer_rate = 0.7

ORDER = (
    (0, 1, 0), (0, 3, 0), (1, 0, 0), (0, 2, 0), (1, 1, 0), (1, 3, 0), (1, 2, 0),
    (0, 1, 1), (0, 3, 1), (1, 0, 1), (0, 2, 1), (1, 1, 1), (1, 3, 1), (1, 2, 1),
    (0, 0, 1),
)


def number(offset):
    return (offset[0] * 4 + offset[1]) * 2 + offset[2]


def path_at(me, offset, sign):
    x, y, c = me // 8, (me // 2) % 4, me % 2
    x = (x + offset[0]) % 2
    y = (y + sign * offset[1] + 4) % 4
    c = (c + offset[2]) % 2
    return (x * 4 + y) * 2 + c


def offset_of(index):
    return (index // 8, (index // 2) % 4, index % 2)


def kernel(
    ids_ref, counts_ref, params_ref, global_ref, momentum_ref,
    new_global_ref, new_momentum_ref, placed_ref,
    *scratch, paths, owned, held, shards, rows, chunks, span,
):
    (ids, counts, local, glob, mom, out, raw, squares, mine, others, factor,
     rounded, out_back, new_glob, new_mom, placed, pick_v, table_v, weight_v,
     pick, table, weight) = scratch[:22]
    arrived = scratch[22:22 + chunks]
    back = scratch[22 + chunks:22 + 2 * chunks]
    (load_sem, send_sem, recv_sem, back_sem, norm_send, norm_recv, store_sem) = scratch[22 + 2 * chunks:]
    me = lax.axis_index("path")
    shard = lax.axis_index("shard")
    block = rows // chunks

    load_ids = pltpu.make_async_copy(ids_ref, ids, load_sem.at[0])
    load_counts = pltpu.make_async_copy(counts_ref, counts, load_sem.at[1])
    load_local = pltpu.make_async_copy(params_ref, local, load_sem.at[2])
    load_glob = pltpu.make_async_copy(global_ref, glob, load_sem.at[3])
    load_mom = pltpu.make_async_copy(momentum_ref, mom, load_sem.at[4])
    for load in (load_ids, load_counts, load_local, load_glob, load_mom):
        load.start()
    barrier = pltpu.get_barrier_semaphore()
    for offset in ORDER:
        pl.semaphore_signal(
            barrier, inc=1, device_id=(path_at(me, offset, 1), shard), device_id_type=MESH
        )
    zl = shards // 2
    shard_offsets = [(a, b) for a in range(2) for b in range(zl)][1:]

    def shard_at(a, b):
        return ((shard // zl + a) % 2) * zl + (shard % zl + b) % zl

    for a, b in shard_offsets:
        pl.semaphore_signal(barrier, inc=1, device_id=(me, shard_at(a, b)), device_id_type=MESH)

    lane = lax.broadcasted_iota(jnp.int32, (paths, LANES), 1)
    sub = lax.broadcasted_iota(jnp.int32, (paths, LANES), 0)
    place = lax.broadcasted_iota(jnp.int32, (paths, held), 1)
    load_ids.wait()
    load_counts.wait()
    all_ids = ids[...]
    group = lax.shift_right_logical(all_ids, 4)
    my_group = lax.shift_right_logical(ids[pl.ds(me, 1), :], 4)
    rowid = lax.broadcasted_iota(jnp.int32, (paths, held), 0)
    goes = my_group == rowid
    first = jnp.min(jnp.where(goes, place, held - 1), axis=1, keepdims=True)
    last = jnp.max(jnp.where(goes, place, 0), axis=1, keepdims=True)
    pick_v[...] = jnp.where(lane == 0, first, last)
    copy_pick = pltpu.make_async_copy(pick_v, pick, load_sem.at[0])
    copy_pick.start()

    ours = group == me
    local_ids = all_ids - me * owned
    from_first = jnp.min(jnp.where(ours, place, held - 1), axis=1, keepdims=True)
    from_last = jnp.max(jnp.where(ours, place, 0), axis=1, keepdims=True)
    first_id = jnp.sum(jnp.where(ours & (place == from_first), local_ids, 0), axis=1, keepdims=True)
    last_id = jnp.sum(jnp.where(ours & (place == from_last), local_ids, 0), axis=1, keepdims=True)
    tab = jnp.where(lane == owned, first_id, last_id)
    amount = jnp.zeros((paths, LANES), jnp.float32)
    tokens = counts[...].astype(jnp.float32)
    for m in range(owned):
        same = local_ids == m
        spot = jnp.sum(jnp.where(same, place, 0), axis=1, keepdims=True)
        slot = jnp.where(spot == from_first, 0, 1)
        tab = jnp.where(lane == m, slot, tab)
        amount = jnp.where(
            lane == m, jnp.sum(jnp.where(same, tokens, 0.0), axis=1, keepdims=True), amount
        )
    rank = jnp.sum(jnp.where(goes & (place != first), 1, 0), axis=0, keepdims=True)
    gx = lax.shift_right_logical(my_group, 3)
    gy = lax.shift_right_logical(my_group, 1) & 3
    gc = my_group & 1
    ox = (gx + me // 8) & 1
    oy = ((me // 2) % 4 + 4 - gy) & 3
    oc = (gc + me % 2) & 1
    where_from = ((ox * 4 + oy) * 2 + oc) * CAP + rank
    table_v[0:paths, :] = tab
    table_v[paths:paths + 1, 0:held] = where_from
    sums = jnp.sum(amount, axis=0, keepdims=True)
    weight_v[0:paths, :] = amount
    weight_v[paths:paths + 1, :] = sums
    weight_v[paths + 1:paths + 2, :] = 1.0 / jnp.maximum(sums, 1.0)
    copy_table = pltpu.make_async_copy(table_v, table, load_sem.at[1])
    copy_weight = pltpu.make_async_copy(weight_v, weight, load_sem.at[5])
    copy_table.start()
    copy_weight.start()

    load_local.wait()
    copy_pick.wait()
    for index in (0, *map(number, ORDER)):
        goal = path_at(me, offset_of(index), 1)
        for r in range(CAP):
            k = pick[goal, r]
            for c in range(chunks):
                piece = local[k, c * block:(c + 1) * block, :]
                if index == 0:
                    arrived[c][0, r] = piece
                else:
                    out[c, index, r] = piece
    pl.semaphore_wait(barrier, len(ORDER) + len(shard_offsets))

    def send(source, target, recv, c, offset, sign):
        index = number(offset)
        return pltpu.make_async_remote_copy(
            src_ref=source.at[c, index],
            dst_ref=target[c].at[index],
            send_sem=send_sem.at[c, index],
            recv_sem=recv.at[c, index],
            device_id=(path_at(me, offset, sign), shard),
            device_id_type=MESH,
        )

    for c in range(chunks):
        for offset in ORDER:
            send(out, arrived, recv_sem, c, offset, 1).start()

    copy_table.wait()
    copy_weight.wait()
    load_glob.wait()
    load_mom.wait()
    for c in range(chunks):
        for offset in ORDER:
            send(out, arrived, recv_sem, c, offset, 1).wait_recv()

        def one_sum(m, carry, c=c):
            acc = jnp.zeros((block, LANES), jnp.float32)
            for index in range(paths):
                source = path_at(me, offset_of(index), -1)
                x = arrived[c][index, table[source, m]]
                acc = acc + weight[source, m] * x.astype(jnp.float32)
            part = (weight[paths, m] * glob[m, c * block:(c + 1) * block, :] - acc) * weight[paths + 1, m]
            raw[c, m] = part
            squared = jnp.sum((part * part).reshape(block // 8, 8, LANES), axis=0)
            if c == 0:
                squares[m] = squared
            else:
                squares[m] += squared
            return carry

        lax.fori_loop(0, owned, one_sum, 0)

    mine[...] = jnp.sum(squares[...], axis=1)
    norms = []
    for j, (a, b) in enumerate(shard_offsets):
        norm = pltpu.make_async_remote_copy(
            src_ref=mine,
            dst_ref=others.at[j],
            send_sem=norm_send.at[j],
            recv_sem=norm_recv.at[j],
            device_id=(me, shard_at(a, b)),
            device_id_type=MESH,
        )
        norm.start()
        norms.append(norm)
    for c in range(chunks):
        for offset in ORDER:
            send(out, arrived, recv_sem, c, offset, 1).wait_send()
    for norm in norms:
        norm.wait()
    whole = mine[...]
    for j in range(len(shard_offsets)):
        whole = whole + others[j]
    mean = jnp.sum(whole, axis=1, keepdims=True) / span
    factor[...] = jnp.broadcast_to(
        jnp.minimum(1.0, 1.0 / jnp.sqrt(mean + 1e-06)), (owned, LANES)
    )

    stores = []
    for c in range(chunks):
        here = slice(c * block, (c + 1) * block)

        def update(m, carry, c=c, here=here):
            delta = raw[c, m] * factor[pl.ds(m, 1), :]
            velocity = outer_momentum * mom[m, here, :] + delta
            updated = glob[m, here, :] - outer_rate * (outer_momentum * velocity + delta)
            new_mom[c, m] = velocity
            new_glob[c, m] = updated
            rounded[m] = updated.astype(jnp.bfloat16)
            return carry

        lax.fori_loop(0, owned, update, 0)
        for index in (0, *map(number, ORDER)):
            goal = path_at(me, offset_of(index), 1)
            for r in range(CAP):
                piece = rounded[table[goal, owned + r]]
                if index == 0:
                    back[c][r] = piece
                else:
                    out_back[c, index, r] = piece
        for offset in ORDER:
            index = number(offset)
            pltpu.make_async_remote_copy(
                src_ref=out_back.at[c, index],
                dst_ref=back[c].at[pl.ds(index * CAP, CAP)],
                send_sem=send_sem.at[c, index],
                recv_sem=back_sem.at[c, index],
                device_id=(path_at(me, offset, 1), shard),
                device_id_type=MESH,
            ).start()
        for j, (source, target) in enumerate(((new_glob, new_global_ref), (new_mom, new_momentum_ref))):
            store = pltpu.make_async_copy(
                source.at[c], target.at[:, pl.ds(c * block, block), :], store_sem.at[j, c]
            )
            store.start()
            stores.append(store)

    for c in range(chunks):
        for offset in ORDER:
            index = number(offset)
            pltpu.make_async_remote_copy(
                src_ref=out_back.at[c, index],
                dst_ref=back[c].at[pl.ds(index * CAP, CAP)],
                send_sem=send_sem.at[c, index],
                recv_sem=back_sem.at[c, index],
                device_id=(path_at(me, offset, 1), shard),
                device_id_type=MESH,
            ).wait_recv()
        for k in range(held):
            placed[c, k] = back[c][table[paths, k]]
        store = pltpu.make_async_copy(
            placed.at[c], placed_ref.at[:, pl.ds(c * block, block), :], store_sem.at[2, c]
        )
        store.start()
        stores.append(store)
    for c in range(chunks):
        for offset in ORDER:
            index = number(offset)
            pltpu.make_async_remote_copy(
                src_ref=out_back.at[c, index],
                dst_ref=back[c].at[pl.ds(index * CAP, CAP)],
                send_sem=send_sem.at[c, index],
                recv_sem=back_sem.at[c, index],
                device_id=(path_at(me, offset, 1), shard),
                device_id_type=MESH,
            ).wait_send()
    for store in stores:
        store.wait()


def to_tiles(x):
    n, r, w = x.shape
    return x.reshape(n, r, w // LANES, LANES).transpose(0, 2, 1, 3).reshape(n, r * w // LANES, LANES)


def from_tiles(x, r):
    n, rows, _ = x.shape
    w = rows * LANES // r
    return x.reshape(n, w // LANES, r, LANES).transpose(0, 2, 1, 3).reshape(n, r, w)


def on_device(path_params, global_params, momentum, module_ids, token_counts):
    paths, held = module_ids.shape
    owned, r, width = global_params.shape
    shards = lax.axis_size("shard")
    rows = r * width // LANES
    chunks = CHUNKS
    block = rows // chunks
    bf, f32, i32 = jnp.bfloat16, jnp.float32, jnp.int32
    vmem, smem = pltpu.VMEM, pltpu.SMEM
    dma = pltpu.SemaphoreType.DMA
    hbm = pl.BlockSpec(memory_space=pl.ANY)
    scratch = [
        vmem((paths, held), i32), vmem((paths, held), i32),
        vmem((held, rows, LANES), bf), vmem((owned, rows, LANES), f32), vmem((owned, rows, LANES), f32),
        vmem((chunks, paths, CAP, block, LANES), bf),
        vmem((chunks, owned, block, LANES), f32),
        vmem((owned, 8, LANES), f32), vmem((owned, LANES), f32), vmem((shards - 1, owned, LANES), f32),
        vmem((owned, LANES), f32),
        vmem((owned, block, LANES), bf),
        vmem((chunks, paths, CAP, block, LANES), bf),
        vmem((chunks, owned, block, LANES), f32), vmem((chunks, owned, block, LANES), f32),
        vmem((chunks, held, block, LANES), bf),
        vmem((paths, LANES), i32), vmem((paths + 8, LANES), i32), vmem((paths + 8, LANES), f32),
        smem((paths, LANES), i32), smem((paths + 8, LANES), i32), smem((paths + 8, LANES), f32),
        *[vmem((paths, CAP, block, LANES), bf) for _ in range(chunks)],
        *[vmem((paths * CAP, block, LANES), bf) for _ in range(chunks)],
        dma((6,)), dma((chunks, paths)), dma((chunks, paths)), dma((chunks, paths)),
        dma((shards - 1,)), dma((shards - 1,)), dma((3, chunks)),
    ]
    new_global, new_momentum, placed = pl.pallas_call(
        functools.partial(
            kernel, paths=paths, owned=owned, held=held, shards=shards, rows=rows,
            chunks=chunks, span=r * width * shards,
        ),
        out_shape=(
            jax.ShapeDtypeStruct((owned, rows, LANES), f32),
            jax.ShapeDtypeStruct((owned, rows, LANES), f32),
            jax.ShapeDtypeStruct((held, rows, LANES), bf),
        ),
        in_specs=[hbm] * 5,
        out_specs=(hbm, hbm, hbm),
        scratch_shapes=scratch,
        compiler_params=pltpu.CompilerParams(
            collective_id=0, has_side_effects=True, vmem_limit_bytes=48 * 1024 * 1024
        ),
    )(module_ids, token_counts, to_tiles(path_params[0]), to_tiles(global_params), to_tiles(momentum))
    return (
        from_tiles(new_global, r),
        from_tiles(new_momentum, r),
        from_tiles(placed, r)[None],
    )


def solution(mesh):
    placed = (
        P("path", None, "shard", None),
        P("path", "shard", None),
        P("path", "shard", None),
        P(),
        P(),
    )
    return jax.shard_map(
        on_device,
        mesh=mesh,
        in_specs=placed,
        out_specs=(
            P("path", "shard", None),
            P("path", "shard", None),
            P("path", None, "shard", None),
        ),
        check_vma=False,
    )
```

```python
import functools

import jax
import jax.numpy as jnp
from jax import lax
from jax.experimental import pallas as pl
from jax.experimental.pallas import tpu as pltpu
from jax.sharding import PartitionSpec as P

MESH = pl.DeviceIdType.MESH
CAP = 2
OUT_CHUNKS = (192, 64)
BACK_CHUNKS = (32, 224)
LANES = 128

outer_momentum = 0.9
outer_rate = 0.7
from_past = outer_rate * outer_momentum * outer_momentum
from_delta = outer_rate * (1.0 + outer_momentum)

ORDER = (
    (1, 2, 0), (1, 2, 1), (0, 2, 0), (0, 2, 1), (1, 1, 0), (1, 3, 1), (0, 1, 0), (0, 3, 1),
    (1, 1, 1), (1, 3, 0), (0, 1, 1), (0, 3, 0), (1, 0, 0), (1, 0, 1), (0, 0, 1),
)


def number(offset):
    return (offset[0] * 4 + offset[1]) * 2 + offset[2]


def path_at(me, offset, sign):
    x, y, c = me // 8, (me // 2) % 4, me % 2
    x = (x + offset[0]) % 2
    y = (y + sign * offset[1] + 4) % 4
    c = (c + offset[2]) % 2
    return (x * 4 + y) * 2 + c


def offset_of(index):
    return (index // 8, (index // 2) % 4, index % 2)


def kernel(
    ids_ref, counts_ref, params_ref, global_ref, momentum_ref, new_glob, new_mom, placed,
    *scratch, paths, owned, held, shards, rows, span,
):
    scratch = list(scratch)

    def take(n):
        taken = scratch[:n]
        del scratch[:n]
        return taken

    ids, counts, local, glob, mom, raw, parts, squares, mine, others, factor, rounded = take(12)
    pick_v, table_v, weight_v, pick, table, weight = take(6)
    out, arrived = take(len(OUT_CHUNKS)), take(len(OUT_CHUNKS))
    out_back, back = take(len(BACK_CHUNKS)), take(len(BACK_CHUNKS))
    load_sem, send_sem, recv_sem, send_back_sem, back_sem, norm_send, norm_recv = scratch
    me = lax.axis_index("path")
    shard = lax.axis_index("shard")
    starts = [sum(OUT_CHUNKS[:c]) for c in range(len(OUT_CHUNKS))]
    back_starts = [sum(BACK_CHUNKS[:c]) for c in range(len(BACK_CHUNKS))]

    load_local = pltpu.make_async_copy(params_ref, local, load_sem.at[1])
    load_ids = pltpu.make_async_copy(ids_ref, ids, load_sem.at[2])
    load_counts = pltpu.make_async_copy(counts_ref, counts, load_sem.at[3])
    load_glob = pltpu.make_async_copy(global_ref, glob, load_sem.at[4])
    load_mom = pltpu.make_async_copy(momentum_ref, mom, load_sem.at[5])
    load_ids.start()
    load_local.start()
    barrier = pltpu.get_barrier_semaphore()
    for offset in ORDER:
        pl.semaphore_signal(
            barrier, inc=1, device_id=(path_at(me, offset, 1), shard), device_id_type=MESH
        )
    zl = shards // 2
    shard_offsets = [(a, b) for a in range(2) for b in range(zl)][1:]

    def shard_at(a, b):
        return ((shard // zl + a) % 2) * zl + (shard % zl + b) % zl

    for a, b in shard_offsets:
        pl.semaphore_signal(barrier, inc=1, device_id=(me, shard_at(a, b)), device_id_type=MESH)
    for load in (load_counts, load_glob, load_mom):
        load.start()

    place = lax.broadcasted_iota(jnp.int32, (paths, held), 1)
    lane = lax.broadcasted_iota(jnp.int32, (paths, LANES), 1)
    load_ids.wait()
    my_group = lax.shift_right_logical(ids[pl.ds(me, 1), :], 4)
    goes = my_group == lax.broadcasted_iota(jnp.int32, (paths, held), 0)
    first = jnp.min(jnp.where(goes, place, held - 1), axis=1, keepdims=True)
    last = jnp.max(jnp.where(goes, place, 0), axis=1, keepdims=True)
    pick_v[...] = jnp.where(lane == 0, first, last)
    copy_pick = pltpu.make_async_copy(pick_v, pick, load_sem.at[0])
    copy_pick.start()
    copy_pick.wait()
    load_local.wait()

    def send(c, offset):
        index = number(offset)
        return pltpu.make_async_remote_copy(
            src_ref=out[c].at[index],
            dst_ref=arrived[c].at[pl.ds(index * CAP, CAP)],
            send_sem=send_sem.at[c, index],
            recv_sem=recv_sem.at[c, index],
            device_id=(path_at(me, offset, 1), shard),
            device_id_type=MESH,
        )

    for c, block in enumerate(OUT_CHUNKS):
        for index in (*map(number, ORDER), 0):
            goal = path_at(me, offset_of(index), 1)
            for r in range(CAP):
                piece = local[pick[goal, r], starts[c]:starts[c] + block, :]
                if index == 0:
                    arrived[c][r] = piece
                else:
                    out[c][index, r] = piece
        if c == 0:
            pl.semaphore_wait(barrier, len(ORDER) + len(shard_offsets))
        for offset in ORDER:
            send(c, offset).start()

    slots = CAP * paths
    load_counts.wait()
    all_ids = ids[...]
    ours = lax.shift_right_logical(all_ids, 4) == me
    local_ids = all_ids - me * owned
    tokens = counts[...].astype(jnp.float32)
    from_first = jnp.min(jnp.where(ours, place, held), axis=1, keepdims=True)
    from_last = jnp.max(jnp.where(ours, place, -1), axis=1, keepdims=True)

    def at(spot, x):
        return jnp.sum(jnp.where(ours & (place == spot), x, jnp.zeros_like(x)), axis=1, keepdims=True)

    wide = (paths, LANES)

    def both(a, b):
        return jnp.concatenate([jnp.broadcast_to(a, wide), jnp.broadcast_to(b, wide)], axis=0)

    module = both(at(from_first, local_ids), at(from_last, local_ids))
    amount = both(at(from_first, tokens), at(from_last, tokens))
    valid = both(
        jnp.where(from_last >= 0, 1, 0), jnp.where(from_last > from_first, 1, 0)
    ) > 0
    sub = lax.broadcasted_iota(jnp.int32, (slots, LANES), 0)
    col = lax.broadcasted_iota(jnp.int32, (slots, LANES), 1)

    def across(x):
        return jnp.sum(jnp.where(sub == col, x, 0), axis=0, keepdims=True)

    key = jnp.where(valid, module * slots + sub, slots * owned + sub)
    key_row = across(key)
    module_row = across(jnp.where(valid, module, owned))
    before = (key_row < key) & (col < slots)
    position = jnp.sum(jnp.where(before, 1, 0), axis=1, keepdims=True)
    again = jnp.max(jnp.where(before & (module_row == module), 1.0, 0.0), axis=1, keepdims=True)
    there = position == col
    source = sub & (paths - 1)
    sx = (lax.shift_right_logical(source, 3) + me // 8) & 1
    sy = ((me // 2) % 4 + 4 - (lax.shift_right_logical(source, 1) & 3)) & 3
    sc = ((source & 1) + me % 2) & 1
    landed = ((sx * 4 + sy) * 2 + sc) * CAP + lax.shift_right_logical(sub, 4)
    holds = valid & (module == col)
    total = jnp.sum(jnp.where(holds, amount, 0.0), axis=0, keepdims=True)
    rank = jnp.sum(jnp.where(goes & (place != first), 1, 0), axis=0, keepdims=True)
    ox = (lax.shift_right_logical(my_group, 3) + me // 8) & 1
    oy = ((me // 2) % 4 + 4 - (lax.shift_right_logical(my_group, 1) & 3)) & 3
    oc = ((my_group & 1) + me % 2) & 1
    table_v[0:1, :] = jnp.sum(jnp.where(there, landed, 0), axis=0, keepdims=True)
    table_v[1:2, :] = jnp.max(jnp.where(holds, jnp.broadcast_to(position, holds.shape), 0), axis=0, keepdims=True)
    table_v[2:3, :] = across(jnp.where(valid, module, 0))
    table_v[3:4, 0:held] = ((ox * 4 + oy) * 2 + oc) * CAP + rank
    weight_v[0:1, :] = jnp.sum(jnp.where(there & valid, amount, 0.0), axis=0, keepdims=True)
    weight_v[1:2, :] = jnp.sum(jnp.where(there, jnp.broadcast_to(again, there.shape), 0.0), axis=0, keepdims=True)
    weight_v[2:3, :] = total
    weight_v[3:4, :] = 1.0 / jnp.maximum(total, 1.0)
    weight_v[4:5, :] = jnp.where(total > 0.0, 1.0, 0.0)
    copy_table = pltpu.make_async_copy(table_v, table, load_sem.at[0])
    copy_weight = pltpu.make_async_copy(weight_v, weight, load_sem.at[1])
    copy_table.start()
    copy_weight.start()

    copy_table.wait()
    copy_weight.wait()
    load_glob.wait()
    load_mom.wait()
    for c, block in enumerate(OUT_CHUNKS):
        for offset in ORDER:
            send(c, offset).wait_recv()

        step = min(block, 64)

        for at_row in range(0, block, step):

            def running(e, acc, c=c, step=step, at_row=at_row):
                x = arrived[c][table[0, e], at_row:at_row + step, :].astype(jnp.float32)
                acc = acc * weight[1, e] + x * weight[0, e]
                parts[e, at_row:at_row + step, :] = acc
                return acc

            lax.fori_loop(0, slots, running, jnp.zeros((step, LANES), jnp.float32))

        def one_sum(m, carry, c=c, block=block):
            here = slice(starts[c], starts[c] + block)
            scale = weight[3, m]
            summed = parts[table[1, m], 0:block, :]
            part = glob[m, here, :] * (weight[2, m] * scale) - summed * (weight[4, m] * scale)
            raw[m, here, :] = part
            squared = jnp.sum((part * part).reshape(block // 8, 8, LANES), axis=0)
            if c == 0:
                squares[m] = squared
            else:
                squares[m] += squared
            return carry

        lax.fori_loop(0, owned, one_sum, 0)

    mine[...] = jnp.sum(squares[...], axis=1)
    norms = []
    for j, (a, b) in enumerate(shard_offsets):
        norm = pltpu.make_async_remote_copy(
            src_ref=mine,
            dst_ref=others.at[j],
            send_sem=norm_send.at[j],
            recv_sem=norm_recv.at[j],
            device_id=(me, shard_at(a, b)),
            device_id_type=MESH,
        )
        norm.start()
        norms.append(norm)

    def base(m, carry):
        past = mom[m]
        glob[m] = glob[m] - from_past * past
        mom[m] = outer_momentum * past
        return carry

    lax.fori_loop(0, owned, base, 0)
    for c in range(len(OUT_CHUNKS)):
        for offset in ORDER:
            send(c, offset).wait_send()
    for norm in norms:
        norm.wait()
    whole = mine[...]
    for j in range(len(shard_offsets)):
        whole = whole + others[j]
    mean = jnp.sum(whole, axis=1, keepdims=True) / span
    factor[...] = jnp.broadcast_to(
        jnp.minimum(1.0, 1.0 / jnp.sqrt(mean + 1e-06)), (owned, LANES)
    )

    def send_back(c, offset):
        index = number(offset)
        return pltpu.make_async_remote_copy(
            src_ref=out_back[c].at[index],
            dst_ref=back[c].at[pl.ds(index * CAP, CAP)],
            send_sem=send_back_sem.at[c, index],
            recv_sem=back_sem.at[c, index],
            device_id=(path_at(me, offset, 1), shard),
            device_id_type=MESH,
        )

    for c, block in enumerate(BACK_CHUNKS):

        def update(m, carry, c=c, block=block):
            here = slice(back_starts[c], back_starts[c] + block)
            delta = raw[m, here, :] * factor[pl.ds(m, 1), :]
            updated = glob[m, here, :] - from_delta * delta
            rounded[m, 0:block, :] = updated.astype(jnp.bfloat16)
            new_glob[m, here, :] = updated
            new_mom[m, here, :] = mom[m, here, :] + delta
            return carry

        lax.fori_loop(0, owned, update, 0)
        for index in (*map(number, ORDER), 0):
            goal = path_at(me, offset_of(index), 1)
            for r in range(CAP):
                piece = rounded[table[2, r * paths + goal], 0:block, :]
                if index == 0:
                    back[c][r] = piece
                else:
                    out_back[c][index, r] = piece
        for offset in ORDER:
            send_back(c, offset).start()

    for c, block in enumerate(BACK_CHUNKS):
        for offset in ORDER:
            send_back(c, offset).wait_recv()
        for k in range(held):
            placed[k, back_starts[c]:back_starts[c] + block, :] = back[c][table[3, k]]
    for c in range(len(BACK_CHUNKS)):
        for offset in ORDER:
            send_back(c, offset).wait_send()


def write_out(*refs):
    n = (len(refs) - 1) // 2
    copies = [
        pltpu.make_async_copy(source, target, refs[-1].at[i])
        for i, (source, target) in enumerate(zip(refs[:n], refs[n:2 * n]))
    ]
    for copy in copies:
        copy.start()
    for copy in copies:
        copy.wait()


def to_tiles(x):
    n, r, w = x.shape
    return x.reshape(n, r, w // LANES, LANES).transpose(0, 2, 1, 3).reshape(n, r * w // LANES, LANES)


def from_tiles(x, r):
    n, rows, _ = x.shape
    w = rows * LANES // r
    return x.reshape(n, w // LANES, r, LANES).transpose(0, 2, 1, 3).reshape(n, r, w)


def on_device(path_params, global_params, momentum, module_ids, token_counts):
    paths, held = module_ids.shape
    owned, r, width = global_params.shape
    shards = lax.axis_size("shard")
    rows = r * width // LANES
    bf, f32, i32 = jnp.bfloat16, jnp.float32, jnp.int32
    vmem, smem = pltpu.VMEM, pltpu.SMEM
    dma = pltpu.SemaphoreType.DMA
    in_hbm = pl.BlockSpec(memory_space=pltpu.HBM)
    in_vmem = pl.BlockSpec(memory_space=pltpu.VMEM)
    outs, backs = len(OUT_CHUNKS), len(BACK_CHUNKS)
    scratch = [
        vmem((paths, held), i32), vmem((paths, held), i32),
        vmem((held, rows, LANES), bf), vmem((owned, rows, LANES), f32), vmem((owned, rows, LANES), f32),
        vmem((owned, rows, LANES), f32), vmem((paths * CAP, max(OUT_CHUNKS), LANES), f32),
        vmem((owned, 8, LANES), f32), vmem((owned, LANES), f32), vmem((shards - 1, owned, LANES), f32),
        vmem((owned, LANES), f32),
        vmem((owned, max(BACK_CHUNKS), LANES), bf),
        vmem((paths, LANES), i32), vmem((8, LANES), i32), vmem((8, LANES), f32),
        smem((paths, LANES), i32), smem((8, LANES), i32), smem((8, LANES), f32),
        *[vmem((paths, CAP, block, LANES), bf) for block in OUT_CHUNKS],
        *[vmem((paths * CAP, block, LANES), bf) for block in OUT_CHUNKS],
        *[vmem((paths, CAP, block, LANES), bf) for block in BACK_CHUNKS],
        *[vmem((paths * CAP, block, LANES), bf) for block in BACK_CHUNKS],
        dma((6,)), dma((outs, paths)), dma((outs, paths)), dma((backs, paths)), dma((backs, paths)),
        dma((shards - 1,)), dma((shards - 1,)),
    ]
    shapes = (
        jax.ShapeDtypeStruct((owned, rows, LANES), f32),
        jax.ShapeDtypeStruct((owned, rows, LANES), f32),
        jax.ShapeDtypeStruct((held, rows, LANES), bf),
    )
    results = pl.pallas_call(
        functools.partial(
            kernel, paths=paths, owned=owned, held=held, shards=shards, rows=rows,
            span=r * width * shards,
        ),
        out_shape=shapes,
        in_specs=[in_hbm] * 5,
        out_specs=(in_vmem,) * 3,
        scratch_shapes=scratch,
        compiler_params=pltpu.CompilerParams(
            collective_id=0, has_side_effects=True, vmem_limit_bytes=42 * 1024 * 1024
        ),
    )(*[
        pltpu.with_memory_space_constraint(x, pltpu.HBM)
        for x in (module_ids, token_counts, to_tiles(path_params[0]), to_tiles(global_params), to_tiles(momentum))
    ])
    new_global, new_momentum, placed = pl.pallas_call(
        write_out,
        out_shape=shapes,
        in_specs=[in_vmem] * 3,
        out_specs=(in_hbm,) * 3,
        scratch_shapes=[dma((3,))],
        compiler_params=pltpu.CompilerParams(vmem_limit_bytes=8 * 1024 * 1024),
    )(*results)
    return (
        from_tiles(new_global, r),
        from_tiles(new_momentum, r),
        from_tiles(placed, r)[None],
    )


def solution(mesh):
    placed = (
        P("path", None, "shard", None),
        P("path", "shard", None),
        P("path", "shard", None),
        P(),
        P(),
    )
    return jax.shard_map(
        on_device,
        mesh=mesh,
        in_specs=placed,
        out_specs=(
            P("path", "shard", None),
            P("path", "shard", None),
            P("path", None, "shard", None),
        ),
        check_vma=False,
    )
```

```python
import functools

import jax
import jax.numpy as jnp
from jax import lax
from jax.experimental import pallas as pl
from jax.experimental.pallas import tpu as pltpu
from jax.sharding import PartitionSpec as P

MESH = pl.DeviceIdType.MESH
CAP = 2
OUT_CHUNKS = (192, 64)
BACK_CHUNKS = (32, 224)
LANES = 128
PIECES = 1

outer_momentum = 0.9
outer_rate = 0.7
from_past = outer_rate * outer_momentum * outer_momentum
from_delta = outer_rate * (1.0 + outer_momentum)

CHIPS = ((1, 2), (0, 2), (1, 1), (1, 3), (0, 1), (0, 3), (1, 0))


def number(offset):
    return offset[0] * 4 + offset[1]


def path_at(me, offset, core, sign=1):
    x, y = me // 8, (me // 2) % 4
    return ((x + offset[0]) % 2 * 4 + (y + sign * offset[1] + 4) % 4) * 2 + core


def kernel(
    ids_ref, counts_ref, params_ref, global_ref, momentum_ref, new_glob, new_mom, placed,
    *scratch, paths, owned, held, shards, rows, span,
):
    scratch = list(scratch)

    def take(n):
        taken = scratch[:n]
        del scratch[:n]
        return taken

    ids, counts, local, glob, mom, raw, parts, squares, mine, others, factor, rounded = take(12)
    pick_v, table_v, weight_v, pick, table, weight = take(6)
    out, arrived = take(len(OUT_CHUNKS)), take(len(OUT_CHUNKS))
    out_back, back = take(len(BACK_CHUNKS)), take(len(BACK_CHUNKS))
    load_sem, send_sem, recv_sem, send_back_sem, back_sem, norm_send, norm_recv = scratch
    me = lax.axis_index("path")
    shard = lax.axis_index("shard")
    core = me % 2
    twin = me + 1 - 2 * core
    starts = [sum(OUT_CHUNKS[:c]) for c in range(len(OUT_CHUNKS))]
    back_starts = [sum(BACK_CHUNKS[:c]) for c in range(len(BACK_CHUNKS))]

    load_local = pltpu.make_async_copy(params_ref, local, load_sem.at[1])
    load_ids = pltpu.make_async_copy(ids_ref, ids, load_sem.at[2])
    load_counts = pltpu.make_async_copy(counts_ref, counts, load_sem.at[3])
    load_glob = pltpu.make_async_copy(global_ref, glob, load_sem.at[4])
    load_mom = pltpu.make_async_copy(momentum_ref, mom, load_sem.at[5])
    load_ids.start()
    load_local.start()
    barrier = pltpu.get_barrier_semaphore()
    peers = [path_at(me, offset, other) for offset in CHIPS for other in range(2)] + [twin]
    for peer in peers:
        pl.semaphore_signal(barrier, inc=1, device_id=(peer, shard), device_id_type=MESH)
    zl = shards // 2
    shard_offsets = [(a, b) for a in range(2) for b in range(zl)][1:]

    def shard_at(a, b):
        return ((shard // zl + a) % 2) * zl + (shard % zl + b) % zl

    for a, b in shard_offsets:
        pl.semaphore_signal(barrier, inc=1, device_id=(me, shard_at(a, b)), device_id_type=MESH)
    for load in (load_counts, load_glob, load_mom):
        load.start()

    place = lax.broadcasted_iota(jnp.int32, (paths, held), 1)
    lane = lax.broadcasted_iota(jnp.int32, (paths, LANES), 1)
    load_ids.wait()
    my_group = lax.shift_right_logical(ids[pl.ds(me, 1), :], 4)
    goes = my_group == lax.broadcasted_iota(jnp.int32, (paths, held), 0)
    first = jnp.min(jnp.where(goes, place, held - 1), axis=1, keepdims=True)
    last = jnp.max(jnp.where(goes, place, 0), axis=1, keepdims=True)
    pick_v[...] = jnp.where(lane == 0, first, last)
    copy_pick = pltpu.make_async_copy(pick_v, pick, load_sem.at[0])
    copy_pick.start()
    copy_pick.wait()
    load_local.wait()

    def sent(source, target, send_sems, recv_sems, c, offset, to):
        at_home = 0 if offset is None else number(offset) * 2 + to
        landing = core if offset is None else number(offset) * 2 + core
        goal = twin if offset is None else path_at(me, offset, to)
        return pltpu.make_async_remote_copy(
            src_ref=source[c].at[at_home],
            dst_ref=target[c].at[pl.ds(landing * CAP, CAP)],
            send_sem=send_sems.at[c, at_home],
            recv_sem=recv_sems.at[c, landing],
            device_id=(goal, shard),
            device_id_type=MESH,
        )

    def awaited(source, target, send_sems, recv_sems, c):
        for offset in CHIPS:
            for other in range(2):
                landing = number(offset) * 2 + other
                pltpu.make_async_remote_copy(
                    src_ref=source[c].at[landing],
                    dst_ref=target[c].at[pl.ds(landing * CAP, CAP)],
                    send_sem=send_sems.at[c, landing],
                    recv_sem=recv_sems.at[c, landing],
                    device_id=(path_at(me, offset, other), shard),
                    device_id_type=MESH,
                ).wait_recv()
        landing = 1 - core
        pltpu.make_async_remote_copy(
            src_ref=source[c].at[0],
            dst_ref=target[c].at[pl.ds(landing * CAP, CAP)],
            send_sem=send_sems.at[c, 0],
            recv_sem=recv_sems.at[c, landing],
            device_id=(twin, shard),
            device_id_type=MESH,
        ).wait_recv()

    there_and = (out, arrived, send_sem, recv_sem)
    and_back = (out_back, back, send_back_sem, back_sem)

    def send_half(blocks, to):
        for c in range(len(OUT_CHUNKS)):
            for offset, _ in blocks:
                sent(*there_and, c, offset, to).start()

    for to in range(2):
        blocks = [(offset, to) for offset in CHIPS]
        if to == 0:
            blocks = [(None, None)] + blocks
        for c, block in enumerate(OUT_CHUNKS):
            here = slice(starts[c], starts[c] + block)
            for offset, _ in blocks:
                goal = twin if offset is None else path_at(me, offset, to)
                at_home = 0 if offset is None else number(offset) * 2 + to
                for r in range(CAP):
                    out[c][at_home, r] = local[pick[goal, r], here, :]
        if to == 0:
            pl.semaphore_wait(barrier, len(peers) + len(shard_offsets))
            send_half(blocks, to)
        else:
            pl.when(core == 1)(functools.partial(send_half, blocks, to))
    for c, block in enumerate(OUT_CHUNKS):
        for r in range(CAP):
            arrived[c][core * CAP + r] = local[pick[me, r], starts[c]:starts[c] + block, :]

    slots = CAP * paths
    load_counts.wait()
    all_ids = ids[...]
    ours = lax.shift_right_logical(all_ids, 4) == me
    local_ids = all_ids - me * owned
    tokens = counts[...].astype(jnp.float32)
    from_first = jnp.min(jnp.where(ours, place, held), axis=1, keepdims=True)
    from_last = jnp.max(jnp.where(ours, place, -1), axis=1, keepdims=True)

    def at(spot, x):
        return jnp.sum(jnp.where(ours & (place == spot), x, jnp.zeros_like(x)), axis=1, keepdims=True)

    wide = (paths, LANES)

    def both(a, b):
        return jnp.concatenate([jnp.broadcast_to(a, wide), jnp.broadcast_to(b, wide)], axis=0)

    module = both(at(from_first, local_ids), at(from_last, local_ids))
    amount = both(at(from_first, tokens), at(from_last, tokens))
    valid = both(
        jnp.where(from_last >= 0, 1, 0), jnp.where(from_last > from_first, 1, 0)
    ) > 0
    sub = lax.broadcasted_iota(jnp.int32, (slots, LANES), 0)
    col = lax.broadcasted_iota(jnp.int32, (slots, LANES), 1)

    def across(x):
        return jnp.sum(jnp.where(sub == col, x, 0), axis=0, keepdims=True)

    key = jnp.where(valid, module * slots + sub, slots * owned + sub)
    key_row = across(key)
    module_row = across(jnp.where(valid, module, owned))
    before = (key_row < key) & (col < slots)
    position = jnp.sum(jnp.where(before, 1, 0), axis=1, keepdims=True)
    again = jnp.max(jnp.where(before & (module_row == module), 1.0, 0.0), axis=1, keepdims=True)
    there = position == col
    source = sub & (paths - 1)
    sx = (lax.shift_right_logical(source, 3) + me // 8) & 1
    sy = ((me // 2) % 4 + 4 - (lax.shift_right_logical(source, 1) & 3)) & 3
    sc = source & 1
    landed = ((sx * 4 + sy) * 2 + sc) * CAP + lax.shift_right_logical(sub, 4)
    holds = valid & (module == col)
    total = jnp.sum(jnp.where(holds, amount, 0.0), axis=0, keepdims=True)
    rank = jnp.sum(jnp.where(goes & (place != first), 1, 0), axis=0, keepdims=True)
    ox = (lax.shift_right_logical(my_group, 3) + me // 8) & 1
    oy = ((me // 2) % 4 + 4 - (lax.shift_right_logical(my_group, 1) & 3)) & 3
    oc = my_group & 1
    table_v[0:1, :] = jnp.sum(jnp.where(there, landed, 0), axis=0, keepdims=True)
    table_v[1:2, :] = jnp.max(jnp.where(holds, jnp.broadcast_to(position, holds.shape), 0), axis=0, keepdims=True)
    table_v[2:3, :] = across(jnp.where(valid, module, 0))
    table_v[3:4, 0:held] = ((ox * 4 + oy) * 2 + oc) * CAP + rank
    weight_v[0:1, :] = jnp.sum(jnp.where(there & valid, amount, 0.0), axis=0, keepdims=True)
    weight_v[1:2, :] = jnp.sum(jnp.where(there, jnp.broadcast_to(again, there.shape), 0.0), axis=0, keepdims=True)
    weight_v[2:3, :] = total
    weight_v[3:4, :] = 1.0 / jnp.maximum(total, 1.0)
    weight_v[4:5, :] = jnp.where(total > 0.0, 1.0, 0.0)
    copy_table = pltpu.make_async_copy(table_v, table, load_sem.at[0])
    copy_weight = pltpu.make_async_copy(weight_v, weight, load_sem.at[1])
    copy_table.start()
    copy_weight.start()

    copy_table.wait()
    copy_weight.wait()
    load_glob.wait()
    load_mom.wait()
    for c, block in enumerate(OUT_CHUNKS):
        awaited(*there_and, c)

        step = min(block, 64)

        for at_row in range(0, block, step):

            def running(e, acc, c=c, step=step, at_row=at_row):
                x = arrived[c][table[0, e], at_row:at_row + step, :].astype(jnp.float32)
                acc = acc * weight[1, e] + x * weight[0, e]
                parts[e, at_row:at_row + step, :] = acc
                return acc

            lax.fori_loop(0, slots, running, jnp.zeros((step, LANES), jnp.float32))

        def one_sum(m, carry, c=c, block=block):
            here = slice(starts[c], starts[c] + block)
            scale = weight[3, m]
            summed = parts[table[1, m], 0:block, :]
            part = glob[m, here, :] * (weight[2, m] * scale) - summed * (weight[4, m] * scale)
            raw[m, here, :] = part
            squared = jnp.sum((part * part).reshape(block // 8, 8, LANES), axis=0)
            if c == 0:
                squares[m] = squared
            else:
                squares[m] += squared
            return carry

        lax.fori_loop(0, owned, one_sum, 0)

    mine[...] = jnp.sum(squares[...], axis=1)
    norms = []
    for j, (a, b) in enumerate(shard_offsets):
        norm = pltpu.make_async_remote_copy(
            src_ref=mine,
            dst_ref=others.at[j],
            send_sem=norm_send.at[j],
            recv_sem=norm_recv.at[j],
            device_id=(me, shard_at(a, b)),
            device_id_type=MESH,
        )
        norm.start()
        norms.append(norm)
    pl.when(core == 0)(functools.partial(send_half, blocks, 1))

    def base(m, carry):
        past = mom[m]
        glob[m] = glob[m] - from_past * past
        mom[m] = outer_momentum * past
        return carry

    lax.fori_loop(0, owned, base, 0)
    for norm in norms:
        norm.wait()
    whole = mine[...]
    for j in range(len(shard_offsets)):
        whole = whole + others[j]
    mean = jnp.sum(whole, axis=1, keepdims=True) / span
    factor[...] = jnp.broadcast_to(
        jnp.minimum(1.0, 1.0 / jnp.sqrt(mean + 1e-06)), (owned, LANES)
    )

    targets = [(offset, to) for offset in CHIPS for to in range(2)] + [(None, None)]
    for c, block in enumerate(BACK_CHUNKS):

        def update(m, carry, c=c, block=block):
            here = slice(back_starts[c], back_starts[c] + block)
            delta = raw[m, here, :] * factor[pl.ds(m, 1), :]
            updated = glob[m, here, :] - from_delta * delta
            rounded[m, 0:block, :] = updated.astype(jnp.bfloat16)
            new_glob[m, here, :] = updated
            new_mom[m, here, :] = mom[m, here, :] + delta
            return carry

        lax.fori_loop(0, owned, update, 0)
        for offset, to in targets:
            goal = twin if offset is None else path_at(me, offset, to)
            at_home = 0 if offset is None else number(offset) * 2 + to
            for r in range(CAP):
                out_back[c][at_home, r] = rounded[table[2, r * paths + goal], 0:block, :]
        for offset, to in targets:
            sent(*and_back, c, offset, to).start()
        for r in range(CAP):
            back[c][core * CAP + r] = rounded[table[2, r * paths + me], 0:block, :]

    for c, block in enumerate(BACK_CHUNKS):
        awaited(*and_back, c)
        for k in range(held):
            placed[k, back_starts[c]:back_starts[c] + block, :] = back[c][table[3, k]]
    for way, chunks in ((there_and, OUT_CHUNKS), (and_back, BACK_CHUNKS)):
        for c in range(len(chunks)):
            for offset, to in targets:
                sent(*way, c, offset, to).wait_send()


def write_out(*refs):
    n = (len(refs) - 1) // 2
    copies = []
    for i, (source, target) in enumerate(zip(refs[:n], refs[n:2 * n])):
        piece = source.shape[0] // PIECES
        for j in range(PIECES):
            here = pl.ds(j * piece, piece)
            copies.append(pltpu.make_async_copy(source.at[here], target.at[here], refs[-1].at[i, j]))
    for copy in copies:
        copy.start()
    for copy in copies:
        copy.wait()


def to_tiles(x):
    n, r, w = x.shape
    return x.reshape(n, r, w // LANES, LANES).transpose(0, 2, 1, 3).reshape(n, r * w // LANES, LANES)


def from_tiles(x, r):
    n, rows, _ = x.shape
    w = rows * LANES // r
    return x.reshape(n, w // LANES, r, LANES).transpose(0, 2, 1, 3).reshape(n, r, w)


def on_device(path_params, global_params, momentum, module_ids, token_counts):
    paths, held = module_ids.shape
    owned, r, width = global_params.shape
    shards = lax.axis_size("shard")
    rows = r * width // LANES
    bf, f32, i32 = jnp.bfloat16, jnp.float32, jnp.int32
    vmem, smem = pltpu.VMEM, pltpu.SMEM
    dma = pltpu.SemaphoreType.DMA
    in_hbm = pl.BlockSpec(memory_space=pltpu.HBM)
    in_vmem = pl.BlockSpec(memory_space=pltpu.VMEM)
    outs, backs = len(OUT_CHUNKS), len(BACK_CHUNKS)
    scratch = [
        vmem((paths, held), i32), vmem((paths, held), i32),
        vmem((held, rows, LANES), bf), vmem((owned, rows, LANES), f32), vmem((owned, rows, LANES), f32),
        vmem((owned, rows, LANES), f32), vmem((paths * CAP, max(OUT_CHUNKS), LANES), f32),
        vmem((owned, 8, LANES), f32), vmem((owned, LANES), f32), vmem((shards - 1, owned, LANES), f32),
        vmem((owned, LANES), f32),
        vmem((owned, max(BACK_CHUNKS), LANES), bf),
        vmem((paths, LANES), i32), vmem((8, LANES), i32), vmem((8, LANES), f32),
        smem((paths, LANES), i32), smem((8, LANES), i32), smem((8, LANES), f32),
        *[vmem((paths, CAP, block, LANES), bf) for block in OUT_CHUNKS],
        *[vmem((paths * CAP, block, LANES), bf) for block in OUT_CHUNKS],
        *[vmem((paths, CAP, block, LANES), bf) for block in BACK_CHUNKS],
        *[vmem((paths * CAP, block, LANES), bf) for block in BACK_CHUNKS],
        dma((6,)), dma((outs, paths)), dma((outs, paths)), dma((backs, paths)), dma((backs, paths)),
        dma((shards - 1,)), dma((shards - 1,)),
    ]
    shapes = (
        jax.ShapeDtypeStruct((owned, rows, LANES), f32),
        jax.ShapeDtypeStruct((owned, rows, LANES), f32),
        jax.ShapeDtypeStruct((held, rows, LANES), bf),
    )
    results = pl.pallas_call(
        functools.partial(
            kernel, paths=paths, owned=owned, held=held, shards=shards, rows=rows,
            span=r * width * shards,
        ),
        out_shape=shapes,
        in_specs=[in_hbm] * 5,
        out_specs=(in_vmem,) * 3,
        scratch_shapes=scratch,
        compiler_params=pltpu.CompilerParams(
            collective_id=0, has_side_effects=True, vmem_limit_bytes=42 * 1024 * 1024
        ),
    )(*[
        pltpu.with_memory_space_constraint(x, pltpu.HBM)
        for x in (module_ids, token_counts, to_tiles(path_params[0]), to_tiles(global_params), to_tiles(momentum))
    ])
    new_global, new_momentum, placed = pl.pallas_call(
        write_out,
        out_shape=shapes,
        in_specs=[in_vmem] * 3,
        out_specs=(in_hbm,) * 3,
        scratch_shapes=[dma((3, PIECES))],
        compiler_params=pltpu.CompilerParams(vmem_limit_bytes=8 * 1024 * 1024),
    )(*results)
    return (
        from_tiles(new_global, r),
        from_tiles(new_momentum, r),
        from_tiles(placed, r)[None],
    )


def solution(mesh):
    placed = (
        P("path", None, "shard", None),
        P("path", "shard", None),
        P("path", "shard", None),
        P(),
        P(),
    )
    return jax.shard_map(
        on_device,
        mesh=mesh,
        in_specs=placed,
        out_specs=(
            P("path", "shard", None),
            P("path", "shard", None),
            P("path", None, "shard", None),
        ),
        check_vma=False,
    )
```

```python
import functools

import jax
import jax.numpy as jnp
from jax import lax
from jax.experimental import pallas as pl
from jax.experimental.pallas import tpu as pltpu
from jax.sharding import PartitionSpec as P

MESH = pl.DeviceIdType.MESH
CAP = 2
OUT_CHUNKS = (192, 64)
BACK_CHUNKS = (32, 224)
LANES = 128
PIECES = 1

outer_momentum = 0.9
outer_rate = 0.7
from_past = outer_rate * outer_momentum * outer_momentum
from_delta = outer_rate * (1.0 + outer_momentum)

NEAR = ((0, 2), (1, 0), (0, 1), (0, 3))
FAR = ((1, 2), (1, 1), (1, 3))
CHIPS = FAR + NEAR


def number(offset):
    return offset[0] * 4 + offset[1]


def path_at(me, offset, core, sign=1):
    x, y = me // 8, (me // 2) % 4
    return ((x + offset[0]) % 2 * 4 + (y + sign * offset[1] + 4) % 4) * 2 + core


def kernel(
    ids_ref, counts_ref, params_ref, global_ref, momentum_ref, new_glob, new_mom, placed,
    *scratch, paths, owned, held, shards, rows, span,
):
    scratch = list(scratch)

    def take(n):
        taken = scratch[:n]
        del scratch[:n]
        return taken

    ids, counts, local, glob, mom, raw, parts, squares, mine, others, factor, rounded = take(12)
    pick_v, table_v, weight_v, pick, table, weight = take(6)
    out, arrived = take(len(OUT_CHUNKS)), take(len(OUT_CHUNKS))
    out_back, back = take(len(BACK_CHUNKS)), take(len(BACK_CHUNKS))
    load_sem, send_sem, recv_sem, send_back_sem, back_sem, norm_send, norm_recv, across_x, across_z = scratch
    me = lax.axis_index("path")
    shard = lax.axis_index("shard")
    core = me % 2
    twin = me + 1 - 2 * core
    starts = [sum(OUT_CHUNKS[:c]) for c in range(len(OUT_CHUNKS))]
    back_starts = [sum(BACK_CHUNKS[:c]) for c in range(len(BACK_CHUNKS))]

    load_local = pltpu.make_async_copy(params_ref, local, load_sem.at[1])
    load_ids = pltpu.make_async_copy(ids_ref, ids, load_sem.at[2])
    load_counts = pltpu.make_async_copy(counts_ref, counts, load_sem.at[3])
    load_glob = pltpu.make_async_copy(global_ref, glob, load_sem.at[4])
    load_mom = pltpu.make_async_copy(momentum_ref, mom, load_sem.at[5])
    load_ids.start()
    load_local.start()
    barrier = pltpu.get_barrier_semaphore()
    near = [path_at(me, offset, other) for offset in NEAR for other in range(2)] + [twin]
    for peer in near:
        pl.semaphore_signal(barrier, inc=1, device_id=(peer, shard), device_id_type=MESH)
    zl = shards // 2
    shard_offsets = [(a, b) for a in range(2) for b in range(zl)][1:]

    def shard_at(a, b):
        return ((shard // zl + a) % 2) * zl + (shard % zl + b) % zl

    near_shards = [offset for offset in shard_offsets if offset != (1, zl // 2)]
    for a, b in near_shards:
        pl.semaphore_signal(barrier, inc=1, device_id=(me, shard_at(a, b)), device_id_type=MESH)
    for load in (load_counts, load_glob, load_mom):
        load.start()

    place = lax.broadcasted_iota(jnp.int32, (paths, held), 1)
    lane = lax.broadcasted_iota(jnp.int32, (paths, LANES), 1)
    load_ids.wait()
    my_group = lax.shift_right_logical(ids[pl.ds(me, 1), :], 4)
    goes = my_group == lax.broadcasted_iota(jnp.int32, (paths, held), 0)
    first = jnp.min(jnp.where(goes, place, held - 1), axis=1, keepdims=True)
    last = jnp.max(jnp.where(goes, place, 0), axis=1, keepdims=True)
    pick_v[...] = jnp.where(lane == 0, first, last)
    copy_pick = pltpu.make_async_copy(pick_v, pick, load_sem.at[0])
    copy_pick.start()
    copy_pick.wait()
    load_local.wait()

    def sent(source, target, send_sems, recv_sems, c, offset, to):
        at_home = 0 if offset is None else number(offset) * 2 + to
        landing = core if offset is None else number(offset) * 2 + core
        goal = twin if offset is None else path_at(me, offset, to)
        return pltpu.make_async_remote_copy(
            src_ref=source[c].at[at_home],
            dst_ref=target[c].at[pl.ds(landing * CAP, CAP)],
            send_sem=send_sems.at[c, at_home],
            recv_sem=recv_sems.at[c, landing],
            device_id=(goal, shard),
            device_id_type=MESH,
        )

    def awaited(source, target, send_sems, recv_sems, c):
        for offset in CHIPS:
            for other in range(2):
                landing = number(offset) * 2 + other
                pltpu.make_async_remote_copy(
                    src_ref=source[c].at[landing],
                    dst_ref=target[c].at[pl.ds(landing * CAP, CAP)],
                    send_sem=send_sems.at[c, landing],
                    recv_sem=recv_sems.at[c, landing],
                    device_id=(path_at(me, offset, other), shard),
                    device_id_type=MESH,
                ).wait_recv()
        landing = 1 - core
        pltpu.make_async_remote_copy(
            src_ref=source[c].at[0],
            dst_ref=target[c].at[pl.ds(landing * CAP, CAP)],
            send_sem=send_sems.at[c, 0],
            recv_sem=recv_sems.at[c, landing],
            device_id=(twin, shard),
            device_id_type=MESH,
        ).wait_recv()

    there_and = (out, arrived, send_sem, recv_sem)
    and_back = (out_back, back, send_back_sem, back_sem)

    def send_half(blocks, to):
        for c in range(len(OUT_CHUNKS)):
            for offset in blocks:
                sent(*there_and, c, offset, to).start()

    for to in range(2):
        blocks = [*NEAR, *FAR]
        if to == 0:
            blocks = [None] + blocks
        for c, block in enumerate(OUT_CHUNKS):
            here = slice(starts[c], starts[c] + block)
            for offset in blocks:
                goal = twin if offset is None else path_at(me, offset, to)
                at_home = 0 if offset is None else number(offset) * 2 + to
                for r in range(CAP):
                    out[c][at_home, r] = local[pick[goal, r], here, :]
        if to == 0:
            pl.semaphore_wait(barrier, len(near) + len(near_shards))
            for dy in range(1, 4):
                pl.semaphore_signal(
                    across_x, inc=1, device_id=(path_at(me, (0, dy), core), shard), device_id_type=MESH
                )
            pl.semaphore_signal(
                across_z, inc=1, device_id=(me, shard_at(1, 0)), device_id_type=MESH
            )
            send_half((None, *NEAR), 0)
            pl.semaphore_wait(across_x, 3)
            send_half(FAR, 0)
        else:
            pl.when(core == 1)(functools.partial(send_half, blocks, 1))
    for c, block in enumerate(OUT_CHUNKS):
        for r in range(CAP):
            arrived[c][core * CAP + r] = local[pick[me, r], starts[c]:starts[c] + block, :]

    slots = CAP * paths
    load_counts.wait()
    all_ids = ids[...]
    ours = lax.shift_right_logical(all_ids, 4) == me
    local_ids = all_ids - me * owned
    tokens = counts[...].astype(jnp.float32)
    from_first = jnp.min(jnp.where(ours, place, held), axis=1, keepdims=True)
    from_last = jnp.max(jnp.where(ours, place, -1), axis=1, keepdims=True)

    def at(spot, x):
        return jnp.sum(jnp.where(ours & (place == spot), x, jnp.zeros_like(x)), axis=1, keepdims=True)

    wide = (paths, LANES)

    def both(a, b):
        return jnp.concatenate([jnp.broadcast_to(a, wide), jnp.broadcast_to(b, wide)], axis=0)

    module = both(at(from_first, local_ids), at(from_last, local_ids))
    amount = both(at(from_first, tokens), at(from_last, tokens))
    valid = both(
        jnp.where(from_last >= 0, 1, 0), jnp.where(from_last > from_first, 1, 0)
    ) > 0
    sub = lax.broadcasted_iota(jnp.int32, (slots, LANES), 0)
    col = lax.broadcasted_iota(jnp.int32, (slots, LANES), 1)

    def across(x):
        return jnp.sum(jnp.where(sub == col, x, 0), axis=0, keepdims=True)

    key = jnp.where(valid, module * slots + sub, slots * owned + sub)
    key_row = across(key)
    module_row = across(jnp.where(valid, module, owned))
    before = (key_row < key) & (col < slots)
    position = jnp.sum(jnp.where(before, 1, 0), axis=1, keepdims=True)
    again = jnp.max(jnp.where(before & (module_row == module), 1.0, 0.0), axis=1, keepdims=True)
    there = position == col
    source = sub & (paths - 1)
    sx = (lax.shift_right_logical(source, 3) + me // 8) & 1
    sy = ((me // 2) % 4 + 4 - (lax.shift_right_logical(source, 1) & 3)) & 3
    sc = source & 1
    landed = ((sx * 4 + sy) * 2 + sc) * CAP + lax.shift_right_logical(sub, 4)
    holds = valid & (module == col)
    total = jnp.sum(jnp.where(holds, amount, 0.0), axis=0, keepdims=True)
    rank = jnp.sum(jnp.where(goes & (place != first), 1, 0), axis=0, keepdims=True)
    ox = (lax.shift_right_logical(my_group, 3) + me // 8) & 1
    oy = ((me // 2) % 4 + 4 - (lax.shift_right_logical(my_group, 1) & 3)) & 3
    oc = my_group & 1
    table_v[0:1, :] = jnp.sum(jnp.where(there, landed, 0), axis=0, keepdims=True)
    table_v[1:2, :] = jnp.max(jnp.where(holds, jnp.broadcast_to(position, holds.shape), 0), axis=0, keepdims=True)
    table_v[2:3, :] = across(jnp.where(valid, module, 0))
    table_v[3:4, 0:held] = ((ox * 4 + oy) * 2 + oc) * CAP + rank
    weight_v[0:1, :] = jnp.sum(jnp.where(there & valid, amount, 0.0), axis=0, keepdims=True)
    weight_v[1:2, :] = jnp.sum(jnp.where(there, jnp.broadcast_to(again, there.shape), 0.0), axis=0, keepdims=True)
    weight_v[2:3, :] = total
    weight_v[3:4, :] = 1.0 / jnp.maximum(total, 1.0)
    weight_v[4:5, :] = jnp.where(total > 0.0, 1.0, 0.0)
    copy_table = pltpu.make_async_copy(table_v, table, load_sem.at[0])
    copy_weight = pltpu.make_async_copy(weight_v, weight, load_sem.at[1])
    copy_table.start()
    copy_weight.start()

    copy_table.wait()
    copy_weight.wait()
    load_glob.wait()
    load_mom.wait()
    for c, block in enumerate(OUT_CHUNKS):
        awaited(*there_and, c)

        step = min(block, 64)

        for at_row in range(0, block, step):

            def running(e, acc, c=c, step=step, at_row=at_row):
                x = arrived[c][table[0, e], at_row:at_row + step, :].astype(jnp.float32)
                acc = acc * weight[1, e] + x * weight[0, e]
                parts[e, at_row:at_row + step, :] = acc
                return acc

            lax.fori_loop(0, slots, running, jnp.zeros((step, LANES), jnp.float32))

        def one_sum(m, carry, c=c, block=block):
            here = slice(starts[c], starts[c] + block)
            scale = weight[3, m]
            summed = parts[table[1, m], 0:block, :]
            part = glob[m, here, :] * (weight[2, m] * scale) - summed * (weight[4, m] * scale)
            raw[m, here, :] = part
            squared = jnp.sum((part * part).reshape(block // 8, 8, LANES), axis=0)
            if c == 0:
                squares[m] = squared
            else:
                squares[m] += squared
            return carry

        lax.fori_loop(0, owned, one_sum, 0)

    mine[...] = jnp.sum(squares[...], axis=1)
    pl.semaphore_wait(across_z, 1)
    norms = []
    for j, (a, b) in enumerate(shard_offsets):
        norm = pltpu.make_async_remote_copy(
            src_ref=mine,
            dst_ref=others.at[j],
            send_sem=norm_send.at[j],
            recv_sem=norm_recv.at[j],
            device_id=(me, shard_at(a, b)),
            device_id_type=MESH,
        )
        norm.start()
        norms.append(norm)
    pl.when(core == 0)(functools.partial(send_half, blocks, 1))

    def base(m, carry):
        past = mom[m]
        glob[m] = glob[m] - from_past * past
        mom[m] = outer_momentum * past
        return carry

    lax.fori_loop(0, owned, base, 0)
    for norm in norms:
        norm.wait()
    whole = mine[...]
    for j in range(len(shard_offsets)):
        whole = whole + others[j]
    mean = jnp.sum(whole, axis=1, keepdims=True) / span
    factor[...] = jnp.broadcast_to(
        jnp.minimum(1.0, 1.0 / jnp.sqrt(mean + 1e-06)), (owned, LANES)
    )

    targets = [(offset, to) for offset in CHIPS for to in range(2)] + [(None, None)]
    for c, block in enumerate(BACK_CHUNKS):

        def update(m, carry, c=c, block=block):
            here = slice(back_starts[c], back_starts[c] + block)
            delta = raw[m, here, :] * factor[pl.ds(m, 1), :]
            updated = glob[m, here, :] - from_delta * delta
            rounded[m, 0:block, :] = updated.astype(jnp.bfloat16)
            new_glob[m, here, :] = updated
            new_mom[m, here, :] = mom[m, here, :] + delta
            return carry

        lax.fori_loop(0, owned, update, 0)
        for offset, to in targets:
            goal = twin if offset is None else path_at(me, offset, to)
            at_home = 0 if offset is None else number(offset) * 2 + to
            for r in range(CAP):
                out_back[c][at_home, r] = rounded[table[2, r * paths + goal], 0:block, :]
        for offset, to in targets:
            sent(*and_back, c, offset, to).start()
        for r in range(CAP):
            back[c][core * CAP + r] = rounded[table[2, r * paths + me], 0:block, :]

    for c, block in enumerate(BACK_CHUNKS):
        awaited(*and_back, c)
        for k in range(held):
            placed[k, back_starts[c]:back_starts[c] + block, :] = back[c][table[3, k]]
    for way, chunks in ((there_and, OUT_CHUNKS), (and_back, BACK_CHUNKS)):
        for c in range(len(chunks)):
            for offset, to in targets:
                sent(*way, c, offset, to).wait_send()


def write_out(*refs):
    n = (len(refs) - 1) // 2
    copies = []
    for i, (source, target) in enumerate(zip(refs[:n], refs[n:2 * n])):
        piece = source.shape[0] // PIECES
        for j in range(PIECES):
            here = pl.ds(j * piece, piece)
            copies.append(pltpu.make_async_copy(source.at[here], target.at[here], refs[-1].at[i, j]))
    for copy in copies:
        copy.start()
    for copy in copies:
        copy.wait()


def to_tiles(x):
    n, r, w = x.shape
    return x.reshape(n, r, w // LANES, LANES).transpose(0, 2, 1, 3).reshape(n, r * w // LANES, LANES)


def from_tiles(x, r):
    n, rows, _ = x.shape
    w = rows * LANES // r
    return x.reshape(n, w // LANES, r, LANES).transpose(0, 2, 1, 3).reshape(n, r, w)


def on_device(path_params, global_params, momentum, module_ids, token_counts):
    paths, held = module_ids.shape
    owned, r, width = global_params.shape
    shards = lax.axis_size("shard")
    rows = r * width // LANES
    bf, f32, i32 = jnp.bfloat16, jnp.float32, jnp.int32
    vmem, smem = pltpu.VMEM, pltpu.SMEM
    dma = pltpu.SemaphoreType.DMA
    in_hbm = pl.BlockSpec(memory_space=pltpu.HBM)
    in_vmem = pl.BlockSpec(memory_space=pltpu.VMEM)
    outs, backs = len(OUT_CHUNKS), len(BACK_CHUNKS)
    scratch = [
        vmem((paths, held), i32), vmem((paths, held), i32),
        vmem((held, rows, LANES), bf), vmem((owned, rows, LANES), f32), vmem((owned, rows, LANES), f32),
        vmem((owned, rows, LANES), f32), vmem((paths * CAP, max(OUT_CHUNKS), LANES), f32),
        vmem((owned, 8, LANES), f32), vmem((owned, LANES), f32), vmem((shards - 1, owned, LANES), f32),
        vmem((owned, LANES), f32),
        vmem((owned, max(BACK_CHUNKS), LANES), bf),
        vmem((paths, LANES), i32), vmem((8, LANES), i32), vmem((8, LANES), f32),
        smem((paths, LANES), i32), smem((8, LANES), i32), smem((8, LANES), f32),
        *[vmem((paths, CAP, block, LANES), bf) for block in OUT_CHUNKS],
        *[vmem((paths * CAP, block, LANES), bf) for block in OUT_CHUNKS],
        *[vmem((paths, CAP, block, LANES), bf) for block in BACK_CHUNKS],
        *[vmem((paths * CAP, block, LANES), bf) for block in BACK_CHUNKS],
        dma((6,)), dma((outs, paths)), dma((outs, paths)), dma((backs, paths)), dma((backs, paths)),
        dma((shards - 1,)), dma((shards - 1,)),
        pltpu.SemaphoreType.REGULAR, pltpu.SemaphoreType.REGULAR,
    ]
    shapes = (
        jax.ShapeDtypeStruct((owned, rows, LANES), f32),
        jax.ShapeDtypeStruct((owned, rows, LANES), f32),
        jax.ShapeDtypeStruct((held, rows, LANES), bf),
    )
    results = pl.pallas_call(
        functools.partial(
            kernel, paths=paths, owned=owned, held=held, shards=shards, rows=rows,
            span=r * width * shards,
        ),
        out_shape=shapes,
        in_specs=[in_hbm] * 5,
        out_specs=(in_vmem,) * 3,
        scratch_shapes=scratch,
        compiler_params=pltpu.CompilerParams(
            collective_id=0, has_side_effects=True, vmem_limit_bytes=42 * 1024 * 1024
        ),
    )(*[
        pltpu.with_memory_space_constraint(x, pltpu.HBM)
        for x in (module_ids, token_counts, to_tiles(path_params[0]), to_tiles(global_params), to_tiles(momentum))
    ])
    new_global, new_momentum, placed = pl.pallas_call(
        write_out,
        out_shape=shapes,
        in_specs=[in_vmem] * 3,
        out_specs=(in_hbm,) * 3,
        scratch_shapes=[dma((3, PIECES))],
        compiler_params=pltpu.CompilerParams(vmem_limit_bytes=8 * 1024 * 1024),
    )(*results)
    return (
        from_tiles(new_global, r),
        from_tiles(new_momentum, r),
        from_tiles(placed, r)[None],
    )


def solution(mesh):
    placed = (
        P("path", None, "shard", None),
        P("path", "shard", None),
        P("path", "shard", None),
        P(),
        P(),
    )
    return jax.shard_map(
        on_device,
        mesh=mesh,
        in_specs=placed,
        out_specs=(
            P("path", "shard", None),
            P("path", "shard", None),
            P("path", None, "shard", None),
        ),
        check_vma=False,
    )
```

```python
import functools

import jax
import jax.numpy as jnp
from jax import lax
from jax.experimental import pallas as pl
from jax.experimental.pallas import tpu as pltpu
from jax.sharding import PartitionSpec as P

MESH = pl.DeviceIdType.MESH
CAP = 2
OUT_CHUNKS = (192, 64)
BACK_CHUNKS = (256,)
LANES = 128
PIECES = 1

outer_momentum = 0.9
outer_rate = 0.7
from_past = outer_rate * outer_momentum * outer_momentum
from_delta = outer_rate * (1.0 + outer_momentum)

NEAR = ((0, 2), (1, 0), (0, 1), (0, 3))
FAR = ((1, 2), (1, 1), (1, 3))
CHIPS = FAR + NEAR


def number(offset):
    return offset[0] * 4 + offset[1]


def path_at(me, offset, core, sign=1):
    x, y = me // 8, (me // 2) % 4
    return ((x + offset[0]) % 2 * 4 + (y + sign * offset[1] + 4) % 4) * 2 + core


def kernel(
    ids_ref, counts_ref, params_ref, global_ref, momentum_ref, new_glob, new_mom, placed,
    *scratch, paths, owned, held, shards, rows, span,
):
    scratch = list(scratch)

    def take(n):
        taken = scratch[:n]
        del scratch[:n]
        return taken

    ids, counts, local, glob, mom, raw, parts, squares, mine, others, factor, rounded = take(12)
    pick_v, table_v, weight_v, pick, table, weight = take(6)
    out, arrived = take(len(OUT_CHUNKS)), take(len(OUT_CHUNKS))
    out_back, back = take(len(BACK_CHUNKS)), take(len(BACK_CHUNKS))
    load_sem, send_sem, recv_sem, send_back_sem, back_sem, norm_send, norm_recv, across_x, across_z = scratch
    me = lax.axis_index("path")
    shard = lax.axis_index("shard")
    core = me % 2
    twin = me + 1 - 2 * core
    starts = [sum(OUT_CHUNKS[:c]) for c in range(len(OUT_CHUNKS))]
    back_starts = [sum(BACK_CHUNKS[:c]) for c in range(len(BACK_CHUNKS))]

    load_local = pltpu.make_async_copy(params_ref, local, load_sem.at[1])
    load_ids = pltpu.make_async_copy(ids_ref, ids, load_sem.at[2])
    load_counts = pltpu.make_async_copy(counts_ref, counts, load_sem.at[3])
    load_glob = pltpu.make_async_copy(global_ref, glob, load_sem.at[4])
    load_mom = pltpu.make_async_copy(momentum_ref, mom, load_sem.at[5])
    load_ids.start()
    load_local.start()
    barrier = pltpu.get_barrier_semaphore()
    near = [path_at(me, offset, other) for offset in NEAR for other in range(2)] + [twin]
    for peer in near:
        pl.semaphore_signal(barrier, inc=1, device_id=(peer, shard), device_id_type=MESH)
    zl = shards // 2
    shard_offsets = [(a, b) for a in range(2) for b in range(zl)][1:]

    def shard_at(a, b):
        return ((shard // zl + a) % 2) * zl + (shard % zl + b) % zl

    near_shards = [offset for offset in shard_offsets if offset != (1, zl // 2)]
    for a, b in near_shards:
        pl.semaphore_signal(barrier, inc=1, device_id=(me, shard_at(a, b)), device_id_type=MESH)
    for load in (load_counts, load_glob, load_mom):
        load.start()

    place = lax.broadcasted_iota(jnp.int32, (paths, held), 1)
    lane = lax.broadcasted_iota(jnp.int32, (paths, LANES), 1)
    load_ids.wait()
    my_group = lax.shift_right_logical(ids[pl.ds(me, 1), :], 4)
    goes = my_group == lax.broadcasted_iota(jnp.int32, (paths, held), 0)
    first = jnp.min(jnp.where(goes, place, held - 1), axis=1, keepdims=True)
    last = jnp.max(jnp.where(goes, place, 0), axis=1, keepdims=True)
    pick_v[...] = jnp.where(lane == 0, first, last)
    copy_pick = pltpu.make_async_copy(pick_v, pick, load_sem.at[0])
    copy_pick.start()
    copy_pick.wait()
    load_local.wait()

    def sent(source, target, send_sems, recv_sems, c, offset, to):
        at_home = 0 if offset is None else number(offset) * 2 + to
        landing = core if offset is None else number(offset) * 2 + core
        goal = twin if offset is None else path_at(me, offset, to)
        return pltpu.make_async_remote_copy(
            src_ref=source[c].at[at_home],
            dst_ref=target[c].at[pl.ds(landing * CAP, CAP)],
            send_sem=send_sems.at[c, at_home],
            recv_sem=recv_sems.at[c, landing],
            device_id=(goal, shard),
            device_id_type=MESH,
        )

    def awaited(source, target, send_sems, recv_sems, c):
        for offset in CHIPS:
            for other in range(2):
                landing = number(offset) * 2 + other
                pltpu.make_async_remote_copy(
                    src_ref=source[c].at[landing],
                    dst_ref=target[c].at[pl.ds(landing * CAP, CAP)],
                    send_sem=send_sems.at[c, landing],
                    recv_sem=recv_sems.at[c, landing],
                    device_id=(path_at(me, offset, other), shard),
                    device_id_type=MESH,
                ).wait_recv()
        landing = 1 - core
        pltpu.make_async_remote_copy(
            src_ref=source[c].at[0],
            dst_ref=target[c].at[pl.ds(landing * CAP, CAP)],
            send_sem=send_sems.at[c, 0],
            recv_sem=recv_sems.at[c, landing],
            device_id=(twin, shard),
            device_id_type=MESH,
        ).wait_recv()

    there_and = (out, arrived, send_sem, recv_sem)
    and_back = (out_back, back, send_back_sem, back_sem)

    def send_half(blocks, to):
        for c in range(len(OUT_CHUNKS)):
            for offset in blocks:
                sent(*there_and, c, offset, to).start()

    for to in range(2):
        blocks = [*NEAR, *FAR]
        if to == 0:
            blocks = [None] + blocks
        for c, block in enumerate(OUT_CHUNKS):
            here = slice(starts[c], starts[c] + block)
            for offset in blocks:
                goal = twin if offset is None else path_at(me, offset, to)
                at_home = 0 if offset is None else number(offset) * 2 + to
                for r in range(CAP):
                    out[c][at_home, r] = local[pick[goal, r], here, :]
        if to == 0:
            pl.semaphore_wait(barrier, len(near) + len(near_shards))
            for dy in range(1, 4):
                pl.semaphore_signal(
                    across_x, inc=1, device_id=(path_at(me, (0, dy), core), shard), device_id_type=MESH
                )
            pl.semaphore_signal(
                across_z, inc=1, device_id=(me, shard_at(1, 0)), device_id_type=MESH
            )
            send_half((None, *NEAR), 0)
            pl.semaphore_wait(across_x, 3)
            send_half(FAR, 0)
        else:
            pl.when(core == 1)(functools.partial(send_half, blocks, 1))
    for c, block in enumerate(OUT_CHUNKS):
        for r in range(CAP):
            arrived[c][core * CAP + r] = local[pick[me, r], starts[c]:starts[c] + block, :]

    slots = CAP * paths
    load_counts.wait()
    all_ids = ids[...]
    ours = lax.shift_right_logical(all_ids, 4) == me
    local_ids = all_ids - me * owned
    tokens = counts[...].astype(jnp.float32)
    from_first = jnp.min(jnp.where(ours, place, held), axis=1, keepdims=True)
    from_last = jnp.max(jnp.where(ours, place, -1), axis=1, keepdims=True)

    def at(spot, x):
        return jnp.sum(jnp.where(ours & (place == spot), x, jnp.zeros_like(x)), axis=1, keepdims=True)

    wide = (paths, LANES)

    def both(a, b):
        return jnp.concatenate([jnp.broadcast_to(a, wide), jnp.broadcast_to(b, wide)], axis=0)

    module = both(at(from_first, local_ids), at(from_last, local_ids))
    amount = both(at(from_first, tokens), at(from_last, tokens))
    valid = both(
        jnp.where(from_last >= 0, 1, 0), jnp.where(from_last > from_first, 1, 0)
    ) > 0
    sub = lax.broadcasted_iota(jnp.int32, (slots, LANES), 0)
    col = lax.broadcasted_iota(jnp.int32, (slots, LANES), 1)

    def across(x):
        return jnp.sum(jnp.where(sub == col, x, 0), axis=0, keepdims=True)

    key = jnp.where(valid, module * slots + sub, slots * owned + sub)
    key_row = across(key)
    module_row = across(jnp.where(valid, module, owned))
    before = (key_row < key) & (col < slots)
    position = jnp.sum(jnp.where(before, 1, 0), axis=1, keepdims=True)
    again = jnp.max(jnp.where(before & (module_row == module), 1.0, 0.0), axis=1, keepdims=True)
    there = position == col
    source = sub & (paths - 1)
    sx = (lax.shift_right_logical(source, 3) + me // 8) & 1
    sy = ((me // 2) % 4 + 4 - (lax.shift_right_logical(source, 1) & 3)) & 3
    sc = source & 1
    landed = ((sx * 4 + sy) * 2 + sc) * CAP + lax.shift_right_logical(sub, 4)
    holds = valid & (module == col)
    total = jnp.sum(jnp.where(holds, amount, 0.0), axis=0, keepdims=True)
    rank = jnp.sum(jnp.where(goes & (place != first), 1, 0), axis=0, keepdims=True)
    ox = (lax.shift_right_logical(my_group, 3) + me // 8) & 1
    oy = ((me // 2) % 4 + 4 - (lax.shift_right_logical(my_group, 1) & 3)) & 3
    oc = my_group & 1
    table_v[0:1, :] = jnp.sum(jnp.where(there, landed, 0), axis=0, keepdims=True)
    table_v[1:2, :] = jnp.max(jnp.where(holds, jnp.broadcast_to(position, holds.shape), 0), axis=0, keepdims=True)
    table_v[2:3, :] = across(jnp.where(valid, module, 0))
    table_v[3:4, 0:held] = ((ox * 4 + oy) * 2 + oc) * CAP + rank
    weight_v[0:1, :] = jnp.sum(jnp.where(there & valid, amount, 0.0), axis=0, keepdims=True)
    weight_v[1:2, :] = jnp.sum(jnp.where(there, jnp.broadcast_to(again, there.shape), 0.0), axis=0, keepdims=True)
    weight_v[2:3, :] = total
    weight_v[3:4, :] = 1.0 / jnp.maximum(total, 1.0)
    weight_v[4:5, :] = jnp.where(total > 0.0, 1.0, 0.0)
    copy_table = pltpu.make_async_copy(table_v, table, load_sem.at[0])
    copy_weight = pltpu.make_async_copy(weight_v, weight, load_sem.at[1])
    copy_table.start()
    copy_weight.start()

    copy_table.wait()
    copy_weight.wait()
    load_glob.wait()
    load_mom.wait()
    for c, block in enumerate(OUT_CHUNKS):
        awaited(*there_and, c)

        step = min(block, 64)

        for at_row in range(0, block, step):

            def running(e, acc, c=c, step=step, at_row=at_row):
                x = arrived[c][table[0, e], at_row:at_row + step, :].astype(jnp.float32)
                acc = acc * weight[1, e] + x * weight[0, e]
                parts[e, at_row:at_row + step, :] = acc
                return acc

            lax.fori_loop(0, slots, running, jnp.zeros((step, LANES), jnp.float32), unroll=8)

        def one_sum(m, carry, c=c, block=block, step=step):
            scale = weight[3, m]
            have, want, at = weight[2, m] * scale, weight[4, m] * scale, table[1, m]
            squared = jnp.zeros((8, LANES), jnp.float32)
            for at_row in range(0, block, step):
                here = slice(starts[c] + at_row, starts[c] + at_row + step)
                part = glob[m, here, :] * have - parts[at, at_row:at_row + step, :] * want
                raw[m, here, :] = part
                squared = squared + jnp.sum((part * part).reshape(step // 8, 8, LANES), axis=0)
            if c == 0:
                squares[m] = squared
            else:
                squares[m] += squared
            return carry

        lax.fori_loop(0, owned, one_sum, 0)

    mine[...] = jnp.sum(squares[...], axis=1)
    pl.semaphore_wait(across_z, 1)
    norms = []
    for j, (a, b) in enumerate(shard_offsets):
        norm = pltpu.make_async_remote_copy(
            src_ref=mine,
            dst_ref=others.at[j],
            send_sem=norm_send.at[j],
            recv_sem=norm_recv.at[j],
            device_id=(me, shard_at(a, b)),
            device_id_type=MESH,
        )
        norm.start()
        norms.append(norm)
    pl.when(core == 0)(functools.partial(send_half, blocks, 1))

    def base(m, carry):
        past = mom[m]
        glob[m] = glob[m] - from_past * past
        mom[m] = outer_momentum * past
        return carry

    lax.fori_loop(0, owned, base, 0)
    for norm in norms:
        norm.wait()
    whole = mine[...]
    for j in range(len(shard_offsets)):
        whole = whole + others[j]
    mean = jnp.sum(whole, axis=1, keepdims=True) / span
    factor[...] = jnp.broadcast_to(
        jnp.minimum(1.0, 1.0 / jnp.sqrt(mean + 1e-06)), (owned, LANES)
    )

    targets = [(offset, to) for offset in CHIPS for to in range(2)] + [(None, None)]
    for c, block in enumerate(BACK_CHUNKS):

        def update(m, carry, c=c, block=block):
            here = slice(back_starts[c], back_starts[c] + block)
            delta = raw[m, here, :] * factor[pl.ds(m, 1), :]
            updated = glob[m, here, :] - from_delta * delta
            rounded[m, 0:block, :] = updated.astype(jnp.bfloat16)
            new_glob[m, here, :] = updated
            new_mom[m, here, :] = mom[m, here, :] + delta
            return carry

        lax.fori_loop(0, owned, update, 0)
        for offset, to in targets:
            goal = twin if offset is None else path_at(me, offset, to)
            at_home = 0 if offset is None else number(offset) * 2 + to
            for r in range(CAP):
                out_back[c][at_home, r] = rounded[table[2, r * paths + goal], 0:block, :]
        for offset, to in targets:
            sent(*and_back, c, offset, to).start()
        for r in range(CAP):
            back[c][core * CAP + r] = rounded[table[2, r * paths + me], 0:block, :]

    for c, block in enumerate(BACK_CHUNKS):
        awaited(*and_back, c)
        for k in range(held):
            placed[k, back_starts[c]:back_starts[c] + block, :] = back[c][table[3, k]]
    for way, chunks in ((there_and, OUT_CHUNKS), (and_back, BACK_CHUNKS)):
        for c in range(len(chunks)):
            for offset, to in targets:
                sent(*way, c, offset, to).wait_send()


def write_out(*refs):
    n = (len(refs) - 1) // 2
    copies = []
    for i, (source, target) in enumerate(zip(refs[:n], refs[n:2 * n])):
        piece = source.shape[0] // PIECES
        for j in range(PIECES):
            here = pl.ds(j * piece, piece)
            copies.append(pltpu.make_async_copy(source.at[here], target.at[here], refs[-1].at[i, j]))
    for copy in copies:
        copy.start()
    for copy in copies:
        copy.wait()


def to_tiles(x):
    n, r, w = x.shape
    return x.reshape(n, r, w // LANES, LANES).transpose(0, 2, 1, 3).reshape(n, r * w // LANES, LANES)


def from_tiles(x, r):
    n, rows, _ = x.shape
    w = rows * LANES // r
    return x.reshape(n, w // LANES, r, LANES).transpose(0, 2, 1, 3).reshape(n, r, w)


def on_device(path_params, global_params, momentum, module_ids, token_counts):
    paths, held = module_ids.shape
    owned, r, width = global_params.shape
    shards = lax.axis_size("shard")
    rows = r * width // LANES
    bf, f32, i32 = jnp.bfloat16, jnp.float32, jnp.int32
    vmem, smem = pltpu.VMEM, pltpu.SMEM
    dma = pltpu.SemaphoreType.DMA
    in_hbm = pl.BlockSpec(memory_space=pltpu.HBM)
    in_vmem = pl.BlockSpec(memory_space=pltpu.VMEM)
    outs, backs = len(OUT_CHUNKS), len(BACK_CHUNKS)
    scratch = [
        vmem((paths, held), i32), vmem((paths, held), i32),
        vmem((held, rows, LANES), bf), vmem((owned, rows, LANES), f32), vmem((owned, rows, LANES), f32),
        vmem((owned, rows, LANES), f32), vmem((paths * CAP, max(OUT_CHUNKS), LANES), f32),
        vmem((owned, 8, LANES), f32), vmem((owned, LANES), f32), vmem((shards - 1, owned, LANES), f32),
        vmem((owned, LANES), f32),
        vmem((owned, max(BACK_CHUNKS), LANES), bf),
        vmem((paths, LANES), i32), vmem((8, LANES), i32), vmem((8, LANES), f32),
        smem((paths, LANES), i32), smem((8, LANES), i32), smem((8, LANES), f32),
        *[vmem((paths, CAP, block, LANES), bf) for block in OUT_CHUNKS],
        *[vmem((paths * CAP, block, LANES), bf) for block in OUT_CHUNKS],
        *[vmem((paths, CAP, block, LANES), bf) for block in BACK_CHUNKS],
        *[vmem((paths * CAP, block, LANES), bf) for block in BACK_CHUNKS],
        dma((6,)), dma((outs, paths)), dma((outs, paths)), dma((backs, paths)), dma((backs, paths)),
        dma((shards - 1,)), dma((shards - 1,)),
        pltpu.SemaphoreType.REGULAR, pltpu.SemaphoreType.REGULAR,
    ]
    shapes = (
        jax.ShapeDtypeStruct((owned, rows, LANES), f32),
        jax.ShapeDtypeStruct((owned, rows, LANES), f32),
        jax.ShapeDtypeStruct((held, rows, LANES), bf),
    )
    results = pl.pallas_call(
        functools.partial(
            kernel, paths=paths, owned=owned, held=held, shards=shards, rows=rows,
            span=r * width * shards,
        ),
        out_shape=shapes,
        in_specs=[in_hbm] * 5,
        out_specs=(in_vmem,) * 3,
        scratch_shapes=scratch,
        compiler_params=pltpu.CompilerParams(
            collective_id=0, has_side_effects=True, vmem_limit_bytes=42 * 1024 * 1024
        ),
    )(*[
        pltpu.with_memory_space_constraint(x, pltpu.HBM)
        for x in (module_ids, token_counts, to_tiles(path_params[0]), to_tiles(global_params), to_tiles(momentum))
    ])
    new_global, new_momentum, placed = pl.pallas_call(
        write_out,
        out_shape=shapes,
        in_specs=[in_vmem] * 3,
        out_specs=(in_hbm,) * 3,
        scratch_shapes=[dma((3, PIECES))],
        compiler_params=pltpu.CompilerParams(vmem_limit_bytes=8 * 1024 * 1024),
    )(*results)
    return (
        from_tiles(new_global, r),
        from_tiles(new_momentum, r),
        from_tiles(placed, r)[None],
    )


def solution(mesh):
    placed = (
        P("path", None, "shard", None),
        P("path", "shard", None),
        P("path", "shard", None),
        P(),
        P(),
    )
    return jax.shard_map(
        on_device,
        mesh=mesh,
        in_specs=placed,
        out_specs=(
            P("path", "shard", None),
            P("path", "shard", None),
            P("path", None, "shard", None),
        ),
        check_vma=False,
    )
```

```python
import functools

import jax
import jax.numpy as jnp
from jax import lax
from jax.experimental import pallas as pl
from jax.experimental.pallas import tpu as pltpu
from jax.sharding import PartitionSpec as P

MESH = pl.DeviceIdType.MESH
CAP = 2
OUT_CHUNKS = (192, 64)
BACK_CHUNKS = (256,)
LANES = 128
PIECES = 1

outer_momentum = 0.9
outer_rate = 0.7
from_past = outer_rate * outer_momentum * outer_momentum
from_delta = outer_rate * (1.0 + outer_momentum)

NEAR = ((0, 2), (1, 0), (0, 1), (0, 3))
FAR = ((1, 2), (1, 1), (1, 3))
CHIPS = FAR + NEAR


def number(offset):
    return offset[0] * 4 + offset[1]


def path_at(me, offset, core, sign=1):
    x, y = me // 8, (me // 2) % 4
    return ((x + offset[0]) % 2 * 4 + (y + sign * offset[1] + 4) % 4) * 2 + core


def kernel(
    ids_ref, counts_ref, params_ref, global_ref, momentum_ref, new_glob, new_mom, placed,
    *scratch, paths, owned, held, shards, rows, span,
):
    scratch = list(scratch)

    def take(n):
        taken = scratch[:n]
        del scratch[:n]
        return taken

    ids, counts, local, glob, mom, raw, parts, squares, mine, others, factor, rounded = take(12)
    pick_v, table_v, weight_v, pick, table, weight = take(6)
    out, arrived = take(len(OUT_CHUNKS)), take(len(OUT_CHUNKS))
    out_back, back = take(len(BACK_CHUNKS)), take(len(BACK_CHUNKS))
    load_sem, send_sem, recv_sem, send_back_sem, back_sem, norm_send, norm_recv, across_x, across_z = scratch
    me = lax.axis_index("path")
    shard = lax.axis_index("shard")
    core = me % 2
    twin = me + 1 - 2 * core
    starts = [sum(OUT_CHUNKS[:c]) for c in range(len(OUT_CHUNKS))]
    back_starts = [sum(BACK_CHUNKS[:c]) for c in range(len(BACK_CHUNKS))]

    load_local = pltpu.make_async_copy(params_ref, local, load_sem.at[1])
    load_ids = pltpu.make_async_copy(ids_ref, ids, load_sem.at[2])
    load_counts = pltpu.make_async_copy(counts_ref, counts, load_sem.at[3])
    load_glob = pltpu.make_async_copy(global_ref, glob, load_sem.at[4])
    load_mom = pltpu.make_async_copy(momentum_ref, mom, load_sem.at[5])
    load_ids.start()
    load_local.start()
    barrier = pltpu.get_barrier_semaphore()
    near = [path_at(me, offset, other) for offset in NEAR for other in range(2)] + [twin]
    for peer in near:
        pl.semaphore_signal(barrier, inc=1, device_id=(peer, shard), device_id_type=MESH)
    zl = shards // 2
    shard_offsets = [(a, b) for a in range(2) for b in range(zl)][1:]

    def shard_at(a, b):
        return ((shard // zl + a) % 2) * zl + (shard % zl + b) % zl

    near_shards = [offset for offset in shard_offsets if offset != (1, zl // 2)]
    for a, b in near_shards:
        pl.semaphore_signal(barrier, inc=1, device_id=(me, shard_at(a, b)), device_id_type=MESH)
    for load in (load_counts, load_glob, load_mom):
        load.start()

    place = lax.broadcasted_iota(jnp.int32, (paths, held), 1)
    lane = lax.broadcasted_iota(jnp.int32, (paths, LANES), 1)
    load_ids.wait()
    my_group = lax.shift_right_logical(ids[pl.ds(me, 1), :], 4)
    goes = my_group == lax.broadcasted_iota(jnp.int32, (paths, held), 0)
    first = jnp.min(jnp.where(goes, place, held - 1), axis=1, keepdims=True)
    last = jnp.max(jnp.where(goes, place, 0), axis=1, keepdims=True)
    pick_v[...] = jnp.where(lane == 0, first, last)
    copy_pick = pltpu.make_async_copy(pick_v, pick, load_sem.at[0])
    copy_pick.start()
    copy_pick.wait()
    load_local.wait()

    def sent(source, target, send_sems, recv_sems, c, offset, to):
        at_home = 0 if offset is None else number(offset) * 2 + to
        landing = core if offset is None else number(offset) * 2 + core
        goal = twin if offset is None else path_at(me, offset, to)
        return pltpu.make_async_remote_copy(
            src_ref=source[c].at[at_home],
            dst_ref=target[c].at[pl.ds(landing * CAP, CAP)],
            send_sem=send_sems.at[c, at_home],
            recv_sem=recv_sems.at[c, landing],
            device_id=(goal, shard),
            device_id_type=MESH,
        )

    def awaited(source, target, send_sems, recv_sems, c):
        for offset in CHIPS:
            for other in range(2):
                landing = number(offset) * 2 + other
                pltpu.make_async_remote_copy(
                    src_ref=source[c].at[landing],
                    dst_ref=target[c].at[pl.ds(landing * CAP, CAP)],
                    send_sem=send_sems.at[c, landing],
                    recv_sem=recv_sems.at[c, landing],
                    device_id=(path_at(me, offset, other), shard),
                    device_id_type=MESH,
                ).wait_recv()
        landing = 1 - core
        pltpu.make_async_remote_copy(
            src_ref=source[c].at[0],
            dst_ref=target[c].at[pl.ds(landing * CAP, CAP)],
            send_sem=send_sems.at[c, 0],
            recv_sem=recv_sems.at[c, landing],
            device_id=(twin, shard),
            device_id_type=MESH,
        ).wait_recv()

    there_and = (out, arrived, send_sem, recv_sem)
    and_back = (out_back, back, send_back_sem, back_sem)

    def fill(blocks, to):
        for c, block in enumerate(OUT_CHUNKS):
            here = slice(starts[c], starts[c] + block)
            for offset in blocks:
                goal = twin if offset is None else path_at(me, offset, to)
                at_home = 0 if offset is None else number(offset) * 2 + to
                for r in range(CAP):
                    out[c][at_home, r] = local[pick[goal, r], here, :]

    def send_half(blocks, to):
        for c in range(len(OUT_CHUNKS)):
            for offset in blocks:
                sent(*there_and, c, offset, to).start()

    for to in range(2):
        blocks = [*NEAR, *FAR]
        fill((None, *NEAR) if to == 0 else blocks, to)
        if to == 0:
            pl.semaphore_wait(barrier, len(near) + len(near_shards))
            for dy in range(1, 4):
                pl.semaphore_signal(
                    across_x, inc=1, device_id=(path_at(me, (0, dy), core), shard), device_id_type=MESH
                )
            pl.semaphore_signal(
                across_z, inc=1, device_id=(me, shard_at(1, 0)), device_id_type=MESH
            )
            send_half((None, *NEAR), 0)
            fill(FAR, 0)
            pl.semaphore_wait(across_x, 3)
            send_half(FAR, 0)
        else:
            pl.when(core == 1)(functools.partial(send_half, blocks, 1))
    for c, block in enumerate(OUT_CHUNKS):
        for r in range(CAP):
            arrived[c][core * CAP + r] = local[pick[me, r], starts[c]:starts[c] + block, :]

    slots = CAP * paths
    load_counts.wait()
    all_ids = ids[...]
    ours = lax.shift_right_logical(all_ids, 4) == me
    local_ids = all_ids - me * owned
    tokens = counts[...].astype(jnp.float32)
    from_first = jnp.min(jnp.where(ours, place, held), axis=1, keepdims=True)
    from_last = jnp.max(jnp.where(ours, place, -1), axis=1, keepdims=True)

    def at(spot, x):
        return jnp.sum(jnp.where(ours & (place == spot), x, jnp.zeros_like(x)), axis=1, keepdims=True)

    wide = (paths, LANES)

    def both(a, b):
        return jnp.concatenate([jnp.broadcast_to(a, wide), jnp.broadcast_to(b, wide)], axis=0)

    module = both(at(from_first, local_ids), at(from_last, local_ids))
    amount = both(at(from_first, tokens), at(from_last, tokens))
    valid = both(
        jnp.where(from_last >= 0, 1, 0), jnp.where(from_last > from_first, 1, 0)
    ) > 0
    sub = lax.broadcasted_iota(jnp.int32, (slots, LANES), 0)
    col = lax.broadcasted_iota(jnp.int32, (slots, LANES), 1)

    def across(x):
        return jnp.sum(jnp.where(sub == col, x, 0), axis=0, keepdims=True)

    key = jnp.where(valid, module * slots + sub, slots * owned + sub)
    key_row = across(key)
    module_row = across(jnp.where(valid, module, owned))
    before = (key_row < key) & (col < slots)
    position = jnp.sum(jnp.where(before, 1, 0), axis=1, keepdims=True)
    again = jnp.max(jnp.where(before & (module_row == module), 1.0, 0.0), axis=1, keepdims=True)
    there = position == col
    source = sub & (paths - 1)
    sx = (lax.shift_right_logical(source, 3) + me // 8) & 1
    sy = ((me // 2) % 4 + 4 - (lax.shift_right_logical(source, 1) & 3)) & 3
    sc = source & 1
    landed = ((sx * 4 + sy) * 2 + sc) * CAP + lax.shift_right_logical(sub, 4)
    holds = valid & (module == col)
    total = jnp.sum(jnp.where(holds, amount, 0.0), axis=0, keepdims=True)
    rank = jnp.sum(jnp.where(goes & (place != first), 1, 0), axis=0, keepdims=True)
    ox = (lax.shift_right_logical(my_group, 3) + me // 8) & 1
    oy = ((me // 2) % 4 + 4 - (lax.shift_right_logical(my_group, 1) & 3)) & 3
    oc = my_group & 1
    table_v[0:1, :] = jnp.sum(jnp.where(there, landed, 0), axis=0, keepdims=True)
    table_v[1:2, :] = jnp.max(jnp.where(holds, jnp.broadcast_to(position, holds.shape), 0), axis=0, keepdims=True)
    table_v[2:3, :] = across(jnp.where(valid, module, 0))
    table_v[3:4, 0:held] = ((ox * 4 + oy) * 2 + oc) * CAP + rank
    weight_v[0:1, :] = jnp.sum(jnp.where(there & valid, amount, 0.0), axis=0, keepdims=True)
    weight_v[1:2, :] = jnp.sum(jnp.where(there, jnp.broadcast_to(again, there.shape), 0.0), axis=0, keepdims=True)
    weight_v[2:3, :] = total
    weight_v[3:4, :] = 1.0 / jnp.maximum(total, 1.0)
    weight_v[4:5, :] = jnp.where(total > 0.0, 1.0, 0.0)
    copy_table = pltpu.make_async_copy(table_v, table, load_sem.at[0])
    copy_weight = pltpu.make_async_copy(weight_v, weight, load_sem.at[1])
    copy_table.start()
    copy_weight.start()

    copy_table.wait()
    copy_weight.wait()
    load_glob.wait()
    load_mom.wait()
    for c, block in enumerate(OUT_CHUNKS):
        awaited(*there_and, c)

        step = min(block, 64)

        for at_row in range(0, block, step):

            def running(e, acc, c=c, step=step, at_row=at_row):
                x = arrived[c][table[0, e], at_row:at_row + step, :].astype(jnp.float32)
                acc = acc * weight[1, e] + x * weight[0, e]
                parts[e, at_row:at_row + step, :] = acc
                return acc

            lax.fori_loop(0, slots, running, jnp.zeros((step, LANES), jnp.float32), unroll=8)

        def one_sum(m, carry, c=c, block=block, step=step):
            scale = weight[3, m]
            have, want, at = weight[2, m] * scale, weight[4, m] * scale, table[1, m]
            squared = jnp.zeros((8, LANES), jnp.float32)
            for at_row in range(0, block, step):
                here = slice(starts[c] + at_row, starts[c] + at_row + step)
                part = glob[m, here, :] * have - parts[at, at_row:at_row + step, :] * want
                raw[m, here, :] = part
                squared = squared + jnp.sum((part * part).reshape(step // 8, 8, LANES), axis=0)
            if c == 0:
                squares[m] = squared
            else:
                squares[m] += squared
            return carry

        lax.fori_loop(0, owned, one_sum, 0)

    mine[...] = jnp.sum(squares[...], axis=1)
    pl.semaphore_wait(across_z, 1)
    norms = []
    for j, (a, b) in enumerate(shard_offsets):
        norm = pltpu.make_async_remote_copy(
            src_ref=mine,
            dst_ref=others.at[j],
            send_sem=norm_send.at[j],
            recv_sem=norm_recv.at[j],
            device_id=(me, shard_at(a, b)),
            device_id_type=MESH,
        )
        norm.start()
        norms.append(norm)
    pl.when(core == 0)(functools.partial(send_half, blocks, 1))

    def base(m, carry):
        past = mom[m]
        glob[m] = glob[m] - from_past * past
        mom[m] = outer_momentum * past
        return carry

    lax.fori_loop(0, owned, base, 0)
    for norm in norms:
        norm.wait()
    whole = mine[...]
    for j in range(len(shard_offsets)):
        whole = whole + others[j]
    mean = jnp.sum(whole, axis=1, keepdims=True) / span
    factor[...] = jnp.broadcast_to(
        jnp.minimum(1.0, 1.0 / jnp.sqrt(mean + 1e-06)), (owned, LANES)
    )

    targets = [(offset, to) for offset in CHIPS for to in range(2)] + [(None, None)]
    for c, block in enumerate(BACK_CHUNKS):

        def update(m, carry, c=c, block=block):
            here = slice(back_starts[c], back_starts[c] + block)
            delta = raw[m, here, :] * factor[pl.ds(m, 1), :]
            updated = glob[m, here, :] - from_delta * delta
            rounded[m, 0:block, :] = updated.astype(jnp.bfloat16)
            new_glob[m, here, :] = updated
            new_mom[m, here, :] = mom[m, here, :] + delta
            return carry

        lax.fori_loop(0, owned, update, 0)
        for offset, to in targets:
            goal = twin if offset is None else path_at(me, offset, to)
            at_home = 0 if offset is None else number(offset) * 2 + to
            for r in range(CAP):
                out_back[c][at_home, r] = rounded[table[2, r * paths + goal], 0:block, :]
        for offset, to in targets:
            sent(*and_back, c, offset, to).start()
        for r in range(CAP):
            back[c][core * CAP + r] = rounded[table[2, r * paths + me], 0:block, :]

    for c, block in enumerate(BACK_CHUNKS):
        awaited(*and_back, c)
        for k in range(held):
            placed[k, back_starts[c]:back_starts[c] + block, :] = back[c][table[3, k]]
    for way, chunks in ((there_and, OUT_CHUNKS), (and_back, BACK_CHUNKS)):
        for c in range(len(chunks)):
            for offset, to in targets:
                sent(*way, c, offset, to).wait_send()


def write_out(*refs):
    n = (len(refs) - 1) // 2
    copies = []
    for i, (source, target) in enumerate(zip(refs[:n], refs[n:2 * n])):
        piece = source.shape[0] // PIECES
        for j in range(PIECES):
            here = pl.ds(j * piece, piece)
            copies.append(pltpu.make_async_copy(source.at[here], target.at[here], refs[-1].at[i, j]))
    for copy in copies:
        copy.start()
    for copy in copies:
        copy.wait()


def to_tiles(x):
    n, r, w = x.shape
    return x.reshape(n, r, w // LANES, LANES).transpose(0, 2, 1, 3).reshape(n, r * w // LANES, LANES)


def from_tiles(x, r):
    n, rows, _ = x.shape
    w = rows * LANES // r
    return x.reshape(n, w // LANES, r, LANES).transpose(0, 2, 1, 3).reshape(n, r, w)


def on_device(path_params, global_params, momentum, module_ids, token_counts):
    paths, held = module_ids.shape
    owned, r, width = global_params.shape
    shards = lax.axis_size("shard")
    rows = r * width // LANES
    bf, f32, i32 = jnp.bfloat16, jnp.float32, jnp.int32
    vmem, smem = pltpu.VMEM, pltpu.SMEM
    dma = pltpu.SemaphoreType.DMA
    in_hbm = pl.BlockSpec(memory_space=pltpu.HBM)
    in_vmem = pl.BlockSpec(memory_space=pltpu.VMEM)
    outs, backs = len(OUT_CHUNKS), len(BACK_CHUNKS)
    scratch = [
        vmem((paths, held), i32), vmem((paths, held), i32),
        vmem((held, rows, LANES), bf), vmem((owned, rows, LANES), f32), vmem((owned, rows, LANES), f32),
        vmem((owned, rows, LANES), f32), vmem((paths * CAP, max(OUT_CHUNKS), LANES), f32),
        vmem((owned, 8, LANES), f32), vmem((owned, LANES), f32), vmem((shards - 1, owned, LANES), f32),
        vmem((owned, LANES), f32),
        vmem((owned, max(BACK_CHUNKS), LANES), bf),
        vmem((paths, LANES), i32), vmem((8, LANES), i32), vmem((8, LANES), f32),
        smem((paths, LANES), i32), smem((8, LANES), i32), smem((8, LANES), f32),
        *[vmem((paths, CAP, block, LANES), bf) for block in OUT_CHUNKS],
        *[vmem((paths * CAP, block, LANES), bf) for block in OUT_CHUNKS],
        *[vmem((paths, CAP, block, LANES), bf) for block in BACK_CHUNKS],
        *[vmem((paths * CAP, block, LANES), bf) for block in BACK_CHUNKS],
        dma((6,)), dma((outs, paths)), dma((outs, paths)), dma((backs, paths)), dma((backs, paths)),
        dma((shards - 1,)), dma((shards - 1,)),
        pltpu.SemaphoreType.REGULAR, pltpu.SemaphoreType.REGULAR,
    ]
    shapes = (
        jax.ShapeDtypeStruct((owned, rows, LANES), f32),
        jax.ShapeDtypeStruct((owned, rows, LANES), f32),
        jax.ShapeDtypeStruct((held, rows, LANES), bf),
    )
    results = pl.pallas_call(
        functools.partial(
            kernel, paths=paths, owned=owned, held=held, shards=shards, rows=rows,
            span=r * width * shards,
        ),
        out_shape=shapes,
        in_specs=[in_hbm] * 5,
        out_specs=(in_vmem,) * 3,
        scratch_shapes=scratch,
        compiler_params=pltpu.CompilerParams(
            collective_id=0, has_side_effects=True, vmem_limit_bytes=42 * 1024 * 1024
        ),
    )(*[
        pltpu.with_memory_space_constraint(x, pltpu.HBM)
        for x in (module_ids, token_counts, to_tiles(path_params[0]), to_tiles(global_params), to_tiles(momentum))
    ])
    new_global, new_momentum, placed = pl.pallas_call(
        write_out,
        out_shape=shapes,
        in_specs=[in_vmem] * 3,
        out_specs=(in_hbm,) * 3,
        scratch_shapes=[dma((3, PIECES))],
        compiler_params=pltpu.CompilerParams(vmem_limit_bytes=8 * 1024 * 1024),
    )(*results)
    return (
        from_tiles(new_global, r),
        from_tiles(new_momentum, r),
        from_tiles(placed, r)[None],
    )


def solution(mesh):
    placed = (
        P("path", None, "shard", None),
        P("path", "shard", None),
        P("path", "shard", None),
        P(),
        P(),
    )
    return jax.shard_map(
        on_device,
        mesh=mesh,
        in_specs=placed,
        out_specs=(
            P("path", "shard", None),
            P("path", "shard", None),
            P("path", None, "shard", None),
        ),
        check_vma=False,
    )
```
